256 devices in a mesh: tm: 8 (over y, z_hi), lat: 32 (over x, z_lo, core).
Axes of the slice: x: 4, y: 4, z: 8 (z_hi: 2, z_lo: 4; z = z_hi * 4 + z_lo), core: 2. Of those that a mesh axis runs over, the one named last changes fastest.
Arguments:
- background: bfloat16 [16, 2, 512, 2048], P('tm', None, 'lat'), may hold values from -12 to 12
- conv_weight: bfloat16 [32, 90], replicated, may hold values from -0.625 to 0.625
- conv_bias: float32 [32], replicated, may hold values from -3 to 3
- mix_weight: bfloat16 [32, 32], replicated, may hold values from -1 to 1
- mix_bias: float32 [32], replicated, may hold values from -3 to 3
- out_weight: bfloat16 [2, 32], replicated, may hold values from -0.1875 to 0.1875
- out_bias: float32 [2], replicated, may hold values from -0.3 to 0.3
- drift_east: float32 [512, 2048], P('lat', 'tm'), may hold values from -0.2 to 0.2
- drift_north: float32 [512, 2048], P('lat', 'tm'), may hold values from -0.2 to 0.2
- diffusivity: float32 [512, 2048], P('lat', 'tm'), may hold values from 0.1 to 0.24
- sensors: int32 [16, 32, 8, 128], P(None, 'lat', 'tm'), may hold values from 0 to 4095, as said below
- observations: float32 [16, 32, 8, 2, 128], P(None, 'lat', 'tm'), may hold values from -6 to 6
Outputs:
- total_score: float32 [16, 2, 512, 2048], P('tm', None, 'lat')
The draws below stay inside these ranges and needn't reach their ends.
Inputs may be any that keep to these rules, and one draw needn't show every extreme that they name: `sensors`: each entry is a cell of its tile counted row by row over 16 rows of 256 cells; cells may repeat.
All inputs are finite; a program needn't handle non-finite values.
Results may differ from the reference program's by a relative error of at most 0.0039.
Values may be sent and summed in bfloat16 or wider, within the bound.
A program may use at most 128 MiB of HBM per device.

```python
import jax
import jax.numpy as jnp
from jax import lax

LAT_DEV = 16
LON = 2048
VARS = 2
HID = 32
KT = 5
SUB = 3
SENS = 128
TAPS = 90
FRAMES = 16
LAT = 512
TILE = 256
N_TM = 8
N_LAT = 32


def draw_sensors(key, part):
    shape = (FRAMES, N_LAT, N_TM, SENS)
    keys = jax.random.split(key, 6)
    side = jax.random.randint(keys[0], shape, 0, 4)
    depth = jax.random.randint(keys[1], shape, 0, 2)
    along_row = jax.random.randint(keys[2], shape, 0, TILE)
    along_col = jax.random.randint(keys[3], shape, 0, LAT_DEV)
    picker = jax.random.randint(keys[4], shape, 0, 8)
    anywhere = jax.random.randint(keys[5], shape, 0, LAT_DEV * TILE)
    cell_row = jnp.where(side == 0, depth, jnp.where(side == 1, LAT_DEV - 1 - depth, along_col))
    cell_col = jnp.where(side == 2, depth, jnp.where(side == 3, TILE - 1 - depth, along_row))
    rim_cell = cell_row * TILE + cell_col
    return jnp.where(picker < 7, rim_cell, anywhere).astype(jnp.int32)


def steps_of(rng, extent, pieces, least, high):
    gain, own = 1.0, jax.random.fold_in(rng, 6)
    for position, parts in pieces:
        draws = jnp.exp(jax.random.uniform(jax.random.fold_in(own, position), (parts,), jnp.float32, least / len(pieces), high / len(pieces)))
        gain = gain * jnp.repeat(draws, extent[position] // parts).reshape([-1 if axis == position else 1 for axis in range(len(extent))])
    return gain


def gaussian(stream_key, dims, width, reach, cuts=(), held_as=jnp.bfloat16):
    array = width * jax.random.normal(stream_key, dims, jnp.float32)
    if cuts:
        array = array * steps_of(stream_key, dims, cuts, -0.22, 0.18)
    return jnp.clip(array, -reach, reach).astype(held_as)


def setup_inputs(seed: int = 0) -> dict:
    streams_of = jax.random.split(jax.random.key(seed), 13)
    background = gaussian(streams_of[0], (FRAMES, VARS, LAT, LON), 2.0, 12.0, ((0, 8), (2, 32)))
    conv_weight = gaussian(streams_of[1], (HID, TAPS), TAPS ** -0.5, 0.625)
    conv_bias = gaussian(streams_of[2], (HID,), 0.5, 3.0, (), jnp.float32)
    mix_weight = gaussian(streams_of[3], (HID, HID), HID ** -0.5, 1.0)
    mix_bias = gaussian(streams_of[4], (HID,), 0.5, 3.0, (), jnp.float32)
    out_weight = gaussian(streams_of[5], (VARS, HID), (32 * HID) ** -0.5, 0.1875)
    out_bias = gaussian(streams_of[6], (VARS,), 0.05, 0.3, (), jnp.float32)
    drift_east = jnp.clip(jax.random.uniform(streams_of[7], (LAT, LON), jnp.float32, -0.2, 0.2) * steps_of(streams_of[7], (LAT, LON), ((0, 32), (1, 8)), -0.4, 0.0), -0.2, 0.2)
    drift_north = jnp.clip(jax.random.uniform(streams_of[8], (LAT, LON), jnp.float32, -0.2, 0.2) * steps_of(streams_of[8], (LAT, LON), ((0, 32), (1, 8)), -0.4, 0.0), -0.2, 0.2)
    diffusivity = jnp.clip(0.1 + 0.13999999 * jax.random.uniform(streams_of[9], (LAT, LON), jnp.float32) ** steps_of(streams_of[9], (LAT, LON), ((0, 32), (1, 8)), -0.2, 0.2), 0.1, 0.24)
    sensors = draw_sensors(jax.random.fold_in(streams_of[12], 71), 0)
    observations = gaussian(streams_of[11], (FRAMES, N_LAT, N_TM, VARS, SENS), 1.0, 6.0, ((1, 32), (2, 8)), jnp.float32)
    return {"background": background, "conv_weight": conv_weight, "conv_bias": conv_bias, "mix_weight": mix_weight, "mix_bias": mix_bias, "out_weight": out_weight, "out_bias": out_bias, "drift_east": drift_east, "drift_north": drift_north, "diffusivity": diffusivity, "sensors": sensors, "observations": observations}


def lon_shifted(values, offset):
    return jnp.roll(values, -offset, axis=-1)


def conv_frame(window, conv_weight, conv_bias, mix_weight, mix_bias, out_weight, out_bias):
    row_count = window.shape[2] - 2
    tap_list = []
    for channel in range(window.shape[1]):
        for time_lag in range(window.shape[0]):
            for row_offset in range(3):
                for col_offset in range(3):
                    tap_list.append(lon_shifted(window[time_lag, channel, row_offset:row_offset + row_count], col_offset - 1))
    patches = jnp.stack(tap_list)
    hidden_one = jnp.einsum("hk,kyx->hyx", conv_weight, patches, preferred_element_type=jnp.float32) + conv_bias[:, None, None]
    hidden_one = jax.nn.gelu(hidden_one).astype(jnp.bfloat16)
    hidden_two = jnp.einsum("gh,hyx->gyx", mix_weight, hidden_one, preferred_element_type=jnp.float32) + mix_bias[:, None, None]
    hidden_two = jax.nn.gelu(hidden_two).astype(jnp.bfloat16)
    return jnp.einsum("ch,hyx->cyx", out_weight, hidden_two, preferred_element_type=jnp.float32) + out_bias[:, None, None]


def advance_one_step(values, coefficients):
    center_cell = values[..., 1:-1, 1:-1]
    east_cell = values[..., 1:-1, 2:]
    west_cell = values[..., 1:-1, :-2]
    north_cell = values[..., 2:, 1:-1]
    south_cell = values[..., :-2, 1:-1]
    drift_a = coefficients[0, 0, 1:-1, 1:-1]
    drift_b = coefficients[1, 0, 1:-1, 1:-1]
    diff_k = coefficients[2, 0, 1:-1, 1:-1]
    return (center_cell - drift_a * (east_cell - west_cell) * 0.5 - drift_b * (north_cell - south_cell) * 0.5
            + diff_k * (east_cell + west_cell + north_cell + south_cell - 4.0 * center_cell))


def adjoint_step(values, coefficients):
    drift_a = coefficients[0, 0]
    drift_b = coefficients[1, 0]
    diff_k = coefficients[2, 0]
    from_west = values * (diff_k - 0.5 * drift_a)
    from_east = values * (diff_k + 0.5 * drift_a)
    from_south = values * (diff_k - 0.5 * drift_b)
    from_north = values * (diff_k + 0.5 * drift_b)
    center_cell = values[..., 1:-1, 1:-1]
    return ((1.0 - 4.0 * diff_k[1:-1, 1:-1]) * center_cell + from_west[..., 1:-1, :-2] + from_east[..., 1:-1, 2:]
            + from_south[..., :-2, 1:-1] + from_north[..., 2:, 1:-1])


def pad_field(values, border_width):
    tall_field = jnp.pad(values, [(0, 0)] * (values.ndim - 2) + [(border_width, border_width), (0, 0)])
    return jnp.concatenate([tall_field[..., -border_width:], tall_field, tall_field[..., :border_width]], axis=-1)


def reference(background, conv_weight, conv_bias, mix_weight, mix_bias, out_weight, out_bias,
              drift_east, drift_north, diffusivity, sensors, observations):
    coefficients = jnp.stack([drift_east, drift_north, diffusivity])[:, None]
    widened_coefficients = pad_field(coefficients, 1)
    padded = jnp.pad(background, ((2, 2), (0, 0), (1, 1), (0, 0)))
    tile_cols = LON // N_TM
    tile_row = jnp.arange(N_LAT, dtype=jnp.int32)[None, :, None, None]
    tile_col = jnp.arange(N_TM, dtype=jnp.int32)[None, None, :, None]
    global_row = tile_row * LAT_DEV + sensors // tile_cols
    global_col = tile_col * tile_cols + sensors % tile_cols
    cell_index = (global_row * LON + global_col).reshape(FRAMES, -1)
    obs_rows = observations.transpose(0, 3, 1, 2, 4).reshape(FRAMES, VARS, -1)

    def one_frame(frame_index):
        window = lax.dynamic_slice_in_dim(padded, frame_index, KT, 0)
        prior_score = conv_frame(window, conv_weight, conv_bias, mix_weight, mix_bias, out_weight, out_bias)
        present_values = lax.dynamic_index_in_dim(background, frame_index, 0, False).astype(jnp.float32)
        for step_count in range(SUB):
            present_values = advance_one_step(pad_field(present_values, 1), widened_coefficients)
        flattened_field = present_values.reshape(VARS, -1)
        frame_cells = lax.dynamic_index_in_dim(cell_index, frame_index, 0, False)
        frame_obs = lax.dynamic_index_in_dim(obs_rows, frame_index, 0, False)
        misfit = flattened_field[:, frame_cells] - frame_obs
        diffusion_spread = jnp.zeros_like(flattened_field).at[:, frame_cells].add(misfit).reshape(VARS, LAT, LON)
        for step_count in range(SUB):
            diffusion_spread = adjoint_step(pad_field(diffusion_spread, 1), widened_coefficients)
        return prior_score - diffusion_spread

    return lax.map(one_frame, jnp.arange(FRAMES, dtype=jnp.int32))
```

```python
import functools

import jax
import jax.numpy as jnp
from jax import lax
from jax.experimental import pallas as pl
from jax.experimental.pallas import tpu as pltpu
from jax.sharding import PartitionSpec as P

MESH = pl.DeviceIdType.MESH
F32, BF16, I32 = jnp.float32, jnp.bfloat16, jnp.int32
N_TM = 8
ROWS, LON, TILE = 16, 2048, 256
HID, TAPS, KT, SUB = 32, 90, 5, 3
MID_K = 0.17
CHUNKS = 8
WIDTH = LON // CHUNKS
GELU_A = 1.5957691216057308
GELU_B = 0.2854192627
MAIN, EXTRA = 160, 32
KDIM = MAIN + EXTRA


def gelu_of_twice(y):
    t = jnp.tanh(y * (GELU_A + GELU_B * (y * y)))
    return (y + y * t).astype(BF16)


def iota(shape, dim):
    return lax.broadcasted_iota(I32, shape, dim)


def as_f32(mask):
    return jnp.where(mask, 1.0, 0.0).astype(F32)


def column(row):
    n = row.shape[1]
    eye = iota((n, n), 0) == iota((n, n), 1)
    return jnp.sum(jnp.where(eye, jnp.broadcast_to(row, (n, n)), 0.0), axis=1, keepdims=True)


def build_weights(tm, lat, n_lat, cw, cb, mw, mb, ow, w_sc, mix_sc, mixb_sc, out_sc):
    half_cw = (cw[...].astype(F32) * 0.5).astype(BF16)
    bias = column(cb[...] * 0.5)
    bias_hi = bias.astype(BF16).astype(F32)
    bias_lo = bias - bias_hi
    k = iota((1, KDIM), 1)
    main = k < MAIN
    kk = k - MAIN
    group_h, edge, f_h = kk // 8, (kk // 4) % 2, (kk // 2) % 2
    c = jnp.where(main, (k // 16) % 2, kk % 2)
    row_in = k % 16
    has_prev, has_next = tm > 0, tm < N_TM - 1
    has_south, has_north = lat > 0, lat < n_lat - 1
    bias_row = jnp.where(k == MAIN + 24, 1.0, 0.0).astype(F32) * bias_hi + jnp.where(k == MAIN + 25, 1.0, 0.0).astype(F32) * bias_lo
    expanded = {}
    for t in range(2):
        lag = jnp.where(main, k // 32, 2 * group_h + f_h - t)
        group = (lag + t) // 2
        ok = (lag >= 0) & (lag < KT) & (main | (kk < 24))
        ok = ok & ((group > 0) | has_prev) & ((group < 2) | has_next)
        for j in range(3):
            for i in range(3):
                tap = jnp.where(ok, ((c * KT + lag) * 3 + i) * 3 + j, -1)
                select = as_f32(iota((TAPS, KDIM), 0) == tap).astype(BF16)
                expanded[t, j, i] = jnp.dot(half_cw, select, preferred_element_type=F32)

    def one_row(r, carry):
        spot = [as_f32(main & (row_in == r + i - 1)) for i in range(3)]
        spot[0] = spot[0] + as_f32((~main) & (edge == 0) & (r == 0) & has_south)
        spot[2] = spot[2] + as_f32((~main) & (edge == 1) & (r == ROWS - 1) & has_north)
        for t in range(2):
            for j in range(3):
                val = expanded[t, j, 0] * spot[0] + expanded[t, j, 1] * spot[1] + expanded[t, j, 2] * spot[2]
                if j == 1:
                    val = val + bias_row
                w_sc[t, j, pl.ds(pl.multiple_of(r * HID, HID), HID), :] = val.astype(BF16)
        return carry

    lax.fori_loop(0, ROWS, one_row, 0)
    spread_lanes = as_f32(iota((HID, 8 * HID), 1) % HID == iota((HID, 8 * HID), 0)).astype(BF16)
    lane_row = iota((1, 8 * HID), 1) // HID
    mix_wide = jnp.dot((mw[...].astype(F32) * 0.5).astype(BF16), spread_lanes, preferred_element_type=F32)
    for r in range(8):
        mix_sc[r * HID:(r + 1) * HID, :] = (mix_wide * as_f32(lane_row == r)).astype(BF16)
    mixb_sc[...] = jnp.broadcast_to(column(mb[...] * 0.5), (HID, WIDTH))
    out_wide = jnp.dot(ow[...], spread_lanes, preferred_element_type=F32)
    own_row = iota((16, 8 * HID), 1) // HID == iota((16, 8 * HID), 0) % 8
    first_var = iota((16, 8 * HID), 0) < 8
    both = jnp.where(first_var, jnp.broadcast_to(out_wide[0:1], (16, 8 * HID)), jnp.broadcast_to(out_wide[1:2], (16, 8 * HID)))
    out_sc[...] = jnp.where(own_row, both, 0.0).astype(BF16)


def build_edges(h_sc, hx_sc):
    half = LON // 2
    for hf in range(2):
        parts = []
        for g in range(3):
            for e in range(2):
                parts.append(h_sc[g, e].astype(F32)[hf * 4:hf * 4 + 4, :])
        tail = as_f32(iota((8, half), 0) < 2)
        hx_sc[:, hf * half:(hf + 1) * half] = jnp.concatenate(parts + [tail], axis=0).astype(BF16)


def build_coefficients(lat, n_lat, call_sc, cf_sc):
    for q in range(4):
        live = 1.0
        if q == 0:
            live = jnp.where(lat > 0, 1.0, 0.0).astype(F32)
        if q == 3:
            live = jnp.where(lat < n_lat - 1, 1.0, 0.0).astype(F32)
        for tile in range(N_TM):
            a = call_sc[tile, q, 0].astype(F32) * 0.5
            b = call_sc[tile, q, 1].astype(F32) * 0.5
            k = call_sc[tile, q, 2].astype(F32) + MID_K
            rows, lanes = slice(q * 8, q * 8 + 8), slice(tile * TILE, (tile + 1) * TILE)
            cf_sc[0, rows, lanes] = (1.0 - 4.0 * k) * live
            cf_sc[1, rows, lanes] = (k - a) * live
            cf_sc[2, rows, lanes] = (k + a) * live
            cf_sc[3, rows, lanes] = (k - b) * live
            cf_sc[4, rows, lanes] = (k + b) * live


def build_spread(sens_sc, obs_sc, cnt_sc, os_sc):
    row = iota((32, 128), 0)
    col = iota((TILE, 128), 0)

    def one(n, carry):
        tile, f = n // 2, n % 2
        lanes = pl.ds(pl.multiple_of(tile * TILE, TILE), TILE)
        left, right = [], []
        for side in range(3):
            cell = sens_sc[side, tile, f, 0]
            there = cell // TILE + (side * 16 - 8)
            pick = as_f32(jnp.broadcast_to(there, (32, 128)) == row)
            value = obs_sc[side, tile, f, 0, 0]
            high = value.astype(BF16).astype(F32)
            low = value - high
            left.append(jnp.concatenate([pick, pick * high[0:1], pick * high[1:2], pick * low[0:1], pick * low[1:2]], axis=0).astype(BF16))
            right.append(as_f32(jnp.broadcast_to(cell % TILE, (TILE, 128)) == col).astype(BF16))
        total = jnp.zeros((160, TILE), F32)
        for side in range(3):
            total = total + lax.dot_general(left[side], right[side], (((1,), (1,)), ((), ())), preferred_element_type=F32)
        cnt_sc[f, :, lanes] = total[0:32]
        os_sc[f, 0, :, lanes] = total[32:64] + total[96:128]
        os_sc[f, 1, :, lanes] = total[64:96] + total[128:160]
        return carry

    lax.fori_loop(0, 2 * N_TM, one, 0)


def likelihood(lat, n_lat, xg_sc, halo_sc, cf_sc, cnt_sc, os_sc, adj_sc):
    south = jnp.where(lat > 0, 1.0, 0.0).astype(F32)
    north = jnp.where(lat < n_lat - 1, 1.0, 0.0).astype(F32)

    def one(n, carry):
        f, c = n // 2, n % 2
        u = jnp.concatenate([halo_sc[0, f, c].astype(F32) * south, xg_sc[1, f, c].astype(F32), halo_sc[1, f, c].astype(F32) * north], axis=0)
        for _ in range(SUB):
            u = (cf_sc[0] * u + cf_sc[1] * pltpu.roll(u, LON - 1, 1) + cf_sc[2] * pltpu.roll(u, 1, 1)
                 + cf_sc[3] * pltpu.roll(u, 31, 0) + cf_sc[4] * pltpu.roll(u, 1, 0))
        v = cnt_sc[f] * u - os_sc[f, c]
        for _ in range(SUB):
            v = (cf_sc[0] * v + pltpu.roll(cf_sc[1] * v, 1, 1) + pltpu.roll(cf_sc[2] * v, LON - 1, 1)
                 + pltpu.roll(cf_sc[3] * v, 1, 0) + pltpu.roll(cf_sc[4] * v, 31, 0))
        adj_sc[f, c] = v[8:24]
        return carry

    lax.fori_loop(0, 4, one, 0)


def score_chunk(n, xg_sc, hx_sc, rh_sc, w_sc, mix_sc, mixb_sc, out_sc, ob, adj_sc, out):
    base = pl.multiple_of(n * WIDTH, WIDTH)
    before = pl.multiple_of(lax.rem(n * WIDTH + LON - 128, LON), 128)
    after = pl.multiple_of(lax.rem(n * WIDTH + WIDTH, LON), 128)
    here = pl.ds(base, WIDTH)
    for piece in range(14):
        if piece < 12:
            g, f, c = piece // 4, (piece // 2) % 2, piece % 2
            load = lambda lanes: xg_sc[g, f, c, :, lanes]
        else:
            load = lambda lanes: hx_sc[(piece - 12) * 16:(piece - 11) * 16, lanes]
        rows = slice(piece * 16, piece * 16 + 16)
        mid = load(here)
        prev, nxt = load(pl.ds(before, 128)), load(pl.ds(after, 128))
        rh_sc[0, rows, :] = shift_lanes(jnp.concatenate([prev, mid], axis=1), 1)[:, 128:]
        rh_sc[1, rows, :] = mid
        rh_sc[2, rows, :] = shift_lanes(jnp.concatenate([mid, nxt], axis=1), WIDTH + 127)[:, :WIDTH]
    for t in range(2):
        y = None
        for j in range(3):
            rhs = jnp.concatenate([rh_sc[j, t * 32:t * 32 + MAIN, :], rh_sc[j, 192:224, :]], axis=0)
            part = jnp.dot(w_sc[t, j], rhs, preferred_element_type=F32)
            y = part if y is None else y + part
        first = gelu_of_twice(y)
        for rb in range(2):
            z = jnp.dot(mix_sc[...], first[rb * 256:(rb + 1) * 256], preferred_element_type=F32)
            z = (z.reshape(8, HID, WIDTH) + mixb_sc[...][None]).reshape(256, WIDTH)
            second = gelu_of_twice(z)
            o = jnp.dot(out_sc[...], second, preferred_element_type=F32)
            rows = slice(rb * 8, rb * 8 + 8)
            for c in range(2):
                out[t, c, rows, here] = o[c * 8:c * 8 + 8] + ob[0, c] - adj_sc[t, c, rows, here]


def shift_lanes(x, amount):
    return pltpu.roll(x.astype(F32), amount, 1).astype(BF16)


def kernel(n_lat, bg, sens, obs, de, dn, dk, cw, cb, mw, mb, ow, ob, out,
           xg_sc, e_sc, h_sc, halo_sc, call_sc, sens_sc, obs_sc,
           hx_sc, cf_sc, cnt_sc, os_sc, adj_sc, rh_sc, w_sc, mix_sc, mixb_sc, out_sc,
           loc, s_lat, r_lat, s_tm, r_tm, s_sl, r_sl, s_z, r_z, s_y, r_y, s_c, r_c):
    tm, lat = lax.axis_index("tm"), lax.axis_index("lat")
    z_hi = lax.rem(tm, 2)
    partner = tm + 1 - 2 * z_hi
    step_y = 2 - 4 * z_hi
    onward = lax.rem(tm + step_y + N_TM, N_TM)
    up, down = lax.rem(lat + 1, n_lat), lax.rem(lat + n_lat - 1, n_lat)
    from_partner = 2 - 2 * z_hi
    to_partner = 2 * z_hi

    def remote(src, dst, ss, rs, dev):
        return pltpu.make_async_remote_copy(src_ref=src, dst_ref=dst, send_sem=ss, recv_sem=rs, device_id=dev, device_id_type=MESH)

    own = pltpu.make_async_copy(bg, xg_sc.at[1], loc.at[0])
    own.start()
    own_sens = pltpu.make_async_copy(sens.at[pl.ds(2 * tm, 2)], sens_sc.at[1, tm], loc.at[1])
    own_sens.start()
    own_obs = pltpu.make_async_copy(obs.at[pl.ds(2 * tm, 2)], obs_sc.at[1, tm], loc.at[2])
    own_obs.start()
    for n, ref in enumerate((de, dn, dk)):
        val = ref[...] - (MID_K if n == 2 else 0.0)
        call_sc[tm, 1, n] = val[0:8].astype(BF16)
        call_sc[tm, 2, n] = val[8:16].astype(BF16)
    own.wait()
    half = LON // 2
    for e, row in ((0, 15), (1, 0)):
        rows = [xg_sc[1, f, c].astype(F32)[row:row + 1, :] for f in range(2) for c in range(2)]
        rows = [r[:, :half] for r in rows] + [r[:, half:] for r in rows]
        e_sc[e] = jnp.concatenate(rows, axis=0).astype(BF16)

    barrier = pltpu.get_barrier_semaphore()
    for d in range(1, N_TM):
        pl.semaphore_signal(barrier, inc=1, device_id=(lax.rem(tm + d, N_TM), lat), device_id_type=MESH)
    for other in (up, down):
        pl.semaphore_signal(barrier, inc=1, device_id=(tm, other), device_id_type=MESH)
    pl.semaphore_wait(barrier, N_TM + 1)

    lat_copies = []
    for n, (dev, q_src, q_dst, e, rows) in enumerate(((up, 2, 0, 0, 8), (down, 1, 3, 1, 0))):
        lat_copies.append((
            remote(call_sc.at[tm, q_src], call_sc.at[tm, q_dst], s_lat.at[n, 0], r_lat.at[n, 0], (tm, dev)),
            remote(e_sc.at[e], h_sc.at[1, e], s_lat.at[n, 1], r_lat.at[n, 1], (tm, dev)),
            remote(bg.at[:, :, pl.ds(rows, 8), :], halo_sc.at[n], s_lat.at[n, 2], r_lat.at[n, 2], (tm, dev)),
        ))
    for m in range(2):
        for copies in lat_copies:
            copies[m].start()
    tm_copies = []
    for d in range(1, N_TM):
        to = lax.rem(tm + d, N_TM)
        for m, (src, dst) in enumerate(((sens, sens_sc), (obs, obs_sc))):
            cp = remote(src.at[pl.ds(2 * to, 2)], dst.at[1, tm], s_tm.at[m, d - 1], r_tm.at[m, d - 1], (to, lat))
            cp.start()
            tm_copies.append(cp)
    frames = []
    for n in range(CHUNKS):
        lanes = pl.ds(n * WIDTH, WIDTH)
        frames.append(remote(bg.at[:, :, :, lanes], xg_sc.at[to_partner, :, :, :, lanes], s_z.at[n], r_z.at[n], (partner, lat)))
    for n in range(2):
        frames[n].start()
    for copies in lat_copies:
        copies[2].start()

    for copies in lat_copies:
        copies[0].wait_recv()
    coef_z = remote(call_sc.at[tm], call_sc.at[tm], s_c.at[0], r_c.at[0], (partner, lat))
    coef_z.start()
    for copies in lat_copies:
        copies[1].wait_recv()
    edge_z = remote(h_sc.at[1], h_sc.at[to_partner], s_z.at[CHUNKS], r_z.at[CHUNKS], (partner, lat))
    edge_z.start()
    for n in range(2, CHUNKS):
        frames[n].start()

    build_weights(tm, lat, n_lat, cw, cb, mw, mb, ow, w_sc, mix_sc, mixb_sc, out_sc)

    own_sens.wait()
    own_obs.wait()
    for d in range(1, N_TM):
        frm = lax.rem(tm - d + N_TM, N_TM)
        for m, (src, dst) in enumerate(((sens, sens_sc), (obs, obs_sc))):
            remote(src.at[pl.ds(0, 2)], dst.at[1, frm], s_tm.at[m, d - 1], r_tm.at[m, d - 1], (frm, lat)).wait_recv()
    sensor_copies = []
    for n, (dev, side) in enumerate(((up, 0), (down, 2))):
        for m, ref in enumerate((sens_sc, obs_sc)):
            cp = remote(ref.at[1], ref.at[side], s_sl.at[n, m], r_sl.at[n, m], (tm, dev))
            cp.start()
            sensor_copies.append(cp)

    forwards = []

    def forward(src, dst, n):
        cp = remote(src, dst, s_y.at[n], r_y.at[n], (onward, lat))
        cp.start()
        forwards.append(cp)

    for n in range(2):
        lanes = pl.ds(n * WIDTH, WIDTH)
        frames[n].wait_recv()
        forward(xg_sc.at[from_partner, :, :, :, lanes], xg_sc.at[to_partner, :, :, :, lanes], n)
    pltpu.make_async_remote_copy(src_ref=call_sc.at[partner], dst_ref=call_sc.at[partner], send_sem=s_c.at[0], recv_sem=r_c.at[0],
                                 device_id=(partner, lat), device_id_type=MESH).wait_recv()
    coef_y = []
    pair = pl.ds(tm - z_hi, 2)
    for d in range(1, 4):
        cp = remote(call_sc.at[pair], call_sc.at[pair], s_c.at[d], r_c.at[d], (lax.rem(tm + 2 * d, N_TM), lat))
        cp.start()
        coef_y.append(cp)
    edge_z.wait_recv()
    forward(h_sc.at[from_partner], h_sc.at[to_partner], CHUNKS)
    for n in range(2, CHUNKS):
        lanes = pl.ds(n * WIDTH, WIDTH)
        frames[n].wait_recv()
        forward(xg_sc.at[from_partner, :, :, :, lanes], xg_sc.at[to_partner, :, :, :, lanes], n)
    for cp in sensor_copies:
        cp.wait_recv()
    build_spread(sens_sc, obs_sc, cnt_sc, os_sc)
    for d in range(1, 4):
        there = pl.ds(lax.rem(tm - z_hi - 2 * d + N_TM, N_TM), 2)
        remote(call_sc.at[there], call_sc.at[there], s_c.at[d], r_c.at[d], (lax.rem(tm + 2 * d, N_TM), lat)).wait_recv()
    build_coefficients(lat, n_lat, call_sc, cf_sc)
    for copies in lat_copies:
        copies[2].wait_recv()
    likelihood(lat, n_lat, xg_sc, halo_sc, cf_sc, cnt_sc, os_sc, adj_sc)
    for cp in forwards:
        cp.wait_recv()
    build_edges(h_sc, hx_sc)

    def one_chunk(n, carry):
        score_chunk(n, xg_sc, hx_sc, rh_sc, w_sc, mix_sc, mixb_sc, out_sc, ob, adj_sc, out)
        return carry

    lax.fori_loop(0, CHUNKS, one_chunk, 0)

    for copies in lat_copies:
        for cp in copies:
            cp.wait_send()
    for cp in tm_copies + sensor_copies + frames + [edge_z, coef_z] + forwards + coef_y:
        cp.wait_send()


def solution(mesh):
    n_lat = mesh.shape["lat"]

    def shards(background, conv_weight, conv_bias, mix_weight, mix_bias, out_weight, out_bias,
               drift_east, drift_north, diffusivity, sensors, observations):
        vmem = pl.BlockSpec(memory_space=pltpu.VMEM)
        hbm = pl.BlockSpec(memory_space=pl.ANY)
        smem = pl.BlockSpec(memory_space=pltpu.SMEM)
        dma = pltpu.SemaphoreType.DMA
        scratch = [
            pltpu.VMEM((3, 2, 2, ROWS, LON), BF16),
            pltpu.VMEM((2, 8, LON // 2), BF16),
            pltpu.VMEM((3, 2, 8, LON // 2), BF16),
            pltpu.VMEM((2, 2, 2, 8, LON), BF16),
            pltpu.VMEM((N_TM, 4, 3, 8, TILE), BF16),
            pltpu.VMEM((3, N_TM, 2, 1, 1, 128), I32),
            pltpu.VMEM((3, N_TM, 2, 1, 1, 2, 128), F32),
            pltpu.VMEM((EXTRA, LON), BF16),
            pltpu.VMEM((5, 32, LON), F32),
            pltpu.VMEM((2, 32, LON), F32),
            pltpu.VMEM((2, 2, 32, LON), F32),
            pltpu.VMEM((2, 2, ROWS, LON), F32),
            pltpu.VMEM((3, 224, WIDTH), BF16),
            pltpu.VMEM((2, 3, ROWS * HID, KDIM), BF16),
            pltpu.VMEM((256, 256), BF16),
            pltpu.VMEM((HID, WIDTH), F32),
            pltpu.VMEM((16, 256), BF16),
            dma((3,)), dma((2, 3)), dma((2, 3)), dma((2, 7)), dma((2, 7)), dma((2, 2)), dma((2, 2)),
            dma((CHUNKS + 1,)), dma((CHUNKS + 1,)), dma((CHUNKS + 1,)), dma((CHUNKS + 1,)), dma((4,)), dma((4,)),
        ]
        return pl.pallas_call(
            functools.partial(kernel, n_lat),
            out_shape=jax.ShapeDtypeStruct((2, 2, ROWS, LON), F32),
            in_specs=[hbm, hbm, hbm] + [vmem] * 8 + [smem],
            out_specs=vmem,
            scratch_shapes=scratch,
            compiler_params=pltpu.CompilerParams(collective_id=0, has_side_effects=True, vmem_limit_bytes=56 * 1024 * 1024),
        )(background, sensors, observations, drift_east, drift_north, diffusivity,
          conv_weight, conv_bias.reshape(1, HID), mix_weight, mix_bias.reshape(1, HID), out_weight, out_bias.reshape(1, 2))

    placed = (P("tm", None, "lat", None), P(), P(), P(), P(), P(), P(), P("lat", "tm"), P("lat", "tm"), P("lat", "tm"),
              P(None, "lat", "tm", None), P(None, "lat", "tm", None, None))
    return jax.shard_map(shards, mesh=mesh, in_specs=placed, out_specs=P("tm", None, "lat", None), check_vma=False)
```

```python
import functools

import jax
import jax.numpy as jnp
from jax import lax
from jax.experimental import pallas as pl
from jax.experimental.pallas import tpu as pltpu
from jax.sharding import PartitionSpec as P

MESH = pl.DeviceIdType.MESH
F32, BF16, I32 = jnp.float32, jnp.bfloat16, jnp.int32
N_TM = 8
ROWS, LON, TILE = 16, 2048, 256
HID, TAPS, KT, SUB = 32, 90, 5, 3
MID_K = 0.17
CHUNKS = 8
WIDTH = LON // CHUNKS
GELU_A = 1.5957691216057308
GELU_B = 0.2854192627
MAIN, EXTRA = 160, 32
KDIM = MAIN + EXTRA
PAD = 8
WINDOW = 3


def gelu_of_twice(y):
    t = jnp.tanh(y * (GELU_A + GELU_B * (y * y)))
    return (y + y * t).astype(BF16)


def iota(shape, dim):
    return lax.broadcasted_iota(I32, shape, dim)


def as_f32(mask):
    return jnp.where(mask, 1.0, 0.0).astype(F32)


def column(row):
    n = row.shape[1]
    eye = iota((n, n), 0) == iota((n, n), 1)
    return jnp.sum(jnp.where(eye, jnp.broadcast_to(row, (n, n)), 0.0), axis=1, keepdims=True)


def build_weights(tm, lat, n_lat, cw, cb, mw, mb, ow, w_sc, mix_sc, mixb_sc, out_sc):
    half_cw = (cw[...].astype(F32) * 0.5).astype(BF16)
    bias = column(cb[...] * 0.5)
    bias_hi = bias.astype(BF16).astype(F32)
    bias_lo = bias - bias_hi
    k = iota((1, KDIM), 1)
    main = k < MAIN
    kk = k - MAIN
    group_h, edge, f_h = kk // 8, (kk // 4) % 2, (kk // 2) % 2
    c = jnp.where(main, (k // 16) % 2, kk % 2)
    row_in = k % 16
    has_prev, has_next = tm > 0, tm < N_TM - 1
    has_south, has_north = lat > 0, lat < n_lat - 1
    bias_row = (as_f32(k == MAIN + 24) * bias_hi + as_f32(k == MAIN + 25) * bias_lo).astype(BF16)
    expanded = {}
    for t in range(2):
        lag = jnp.where(main, k // 32, 2 * group_h + f_h - t)
        group = (lag + t) // 2
        ok = (lag >= 0) & (lag < KT) & (main | (kk < 24))
        ok = ok & ((group > 0) | has_prev) & ((group < 2) | has_next)
        offset = iota((TAPS, KDIM), 0) - jnp.where(ok, (c * KT + lag) * 9, 1000)
        for j in range(3):
            for i in range(3):
                select = as_f32(offset == i * 3 + j).astype(BF16)
                expanded[t, j, i] = jnp.dot(half_cw, select, preferred_element_type=F32).astype(BF16)

    def one_row(r, carry):
        spot = [as_f32(main & (row_in == r + i - 1)) for i in range(3)]
        spot[0] = spot[0] + as_f32((~main) & (edge == 0) & (r == 0) & has_south)
        spot[2] = spot[2] + as_f32((~main) & (edge == 1) & (r == ROWS - 1) & has_north)
        spot = [jnp.broadcast_to(p, (HID, KDIM)).astype(BF16) for p in spot]
        for t in range(2):
            for j in range(3):
                val = expanded[t, j, 0] * spot[0] + expanded[t, j, 1] * spot[1] + expanded[t, j, 2] * spot[2]
                if j == 1:
                    val = val + bias_row
                w_sc[t, j, pl.ds(pl.multiple_of(r * HID, HID), HID), :] = val
        return carry

    lax.fori_loop(0, ROWS, one_row, 0)
    spread_lanes = as_f32(iota((HID, 8 * HID), 1) % HID == iota((HID, 8 * HID), 0)).astype(BF16)
    lane_row = iota((1, 8 * HID), 1) // HID
    mix_wide = jnp.dot((mw[...].astype(F32) * 0.5).astype(BF16), spread_lanes, preferred_element_type=F32)
    for r in range(8):
        mix_sc[r * HID:(r + 1) * HID, :] = (mix_wide * as_f32(lane_row == r)).astype(BF16)
    mixb_sc[...] = jnp.broadcast_to(column(mb[...] * 0.5), (HID, WIDTH))
    out_wide = jnp.dot(ow[...], spread_lanes, preferred_element_type=F32)
    own_row = iota((16, 8 * HID), 1) // HID == iota((16, 8 * HID), 0) % 8
    first_var = iota((16, 8 * HID), 0) < 8
    both = jnp.where(first_var, jnp.broadcast_to(out_wide[0:1], (16, 8 * HID)), jnp.broadcast_to(out_wide[1:2], (16, 8 * HID)))
    out_sc[...] = jnp.where(own_row, both, 0.0).astype(BF16)


def build_edges(h_sc, hx_sc):
    half = LON // 2
    for hf in range(2):
        parts = []
        for g in range(3):
            for e in range(2):
                parts.append(h_sc[g, e].astype(F32)[hf * 4:hf * 4 + 4, :])
        tail = as_f32(iota((8, half), 0) < 2)
        hx_sc[:, hf * half:(hf + 1) * half] = jnp.concatenate(parts + [tail], axis=0).astype(BF16)


def build_coefficients(lat, n_lat, call_sc, cf_sc, fields):
    for ref in fields[0] + fields[1]:
        for j in range(LON // 128):
            ref[j, 0:PAD, :] = jnp.zeros((PAD, 128), F32)
            ref[j, PAD + 32:, :] = jnp.zeros((PAD, 128), F32)
    lane = iota((32, 128), 1)
    live = jnp.where(lat > 0, 1.0, 0.0), jnp.where(lat < n_lat - 1, 1.0, 0.0)
    inside = jnp.concatenate([jnp.full((8, 128), live[0], F32), jnp.ones((16, 128), F32), jnp.full((8, 128), live[1], F32)], axis=0)

    def one_tile(j, carry):
        tile, lanes = j // 2, pl.ds(pl.multiple_of(lax.rem(j, 2) * 128, 128), 128)
        a, b, k = (jnp.concatenate([call_sc[tile, q, n, :, lanes].astype(F32) for q in range(4)], axis=0) for n in range(3))
        k = (k + MID_K) * inside
        a = a * (inside * 0.5)
        b = b * (inside * 0.5)
        center = inside - 4.0 * k
        cf_sc[0, 0, j] = center
        cf_sc[0, 1, j] = k - a
        cf_sc[0, 2, j] = k + a
        cf_sc[0, 3, j] = k - b
        cf_sc[0, 4, j] = k + b
        cf_sc[1, 0, j] = center
        cf_sc[1, 3, j] = pltpu.roll(k + b, 31, 0)
        cf_sc[1, 4, j] = pltpu.roll(k - b, 1, 0)
        return carry

    lax.fori_loop(0, LON // 128, one_tile, 0)

    def shifted(j, carry):
        tiles = LON // 128
        after, before = lax.rem(j + 1, tiles), lax.rem(j + tiles - 1, tiles)
        cf_sc[1, 1, j] = jnp.where(lane == 127, pltpu.roll(cf_sc[0, 2, after], 127, 1), pltpu.roll(cf_sc[0, 2, j], 127, 1))
        cf_sc[1, 2, j] = jnp.where(lane == 0, pltpu.roll(cf_sc[0, 1, before], 1, 1), pltpu.roll(cf_sc[0, 1, j], 1, 1))
        return carry

    lax.fori_loop(0, LON // 128, shifted, 0)


def build_spread(sens_sc, obs_sc, cnt_sc, os_sc):
    col = iota((TILE, 128), 0)
    sides = ((0, 8, 0, 8), (1, 16, 8, 0), (2, 8, 24, 0))

    def one(tile, carry):
        for f in range(2):
            for side, count, at, first_row in sides:
                cell = sens_sc[side, tile, f, 0]
                there = lax.shift_right_logical(cell, 8) - first_row
                pick = as_f32(jnp.broadcast_to(there, (count, 128)) == iota((count, 128), 0))
                value = obs_sc[side, tile, f, 0, 0]
                high = value.astype(BF16).astype(F32)
                low = value - high
                left = jnp.concatenate([pick, pick * high[0:1], pick * high[1:2], pick * low[0:1], pick * low[1:2]], axis=0).astype(BF16)
                right = as_f32(jnp.broadcast_to(cell & (TILE - 1), (TILE, 128)) == col).astype(BF16)
                total = lax.dot_general(left, right, (((1,), (1,)), ((), ())), preferred_element_type=F32)
                rows = slice(at, at + count)
                for h in range(2):
                    part = total[:, lanes_of(h)]
                    cnt_sc[f, 2 * tile + h, rows, :] = part[0:count]
                    os_sc[f, 0, 2 * tile + h, rows, :] = part[count:2 * count] + part[3 * count:4 * count]
                    os_sc[f, 1, 2 * tile + h, rows, :] = part[2 * count:3 * count] + part[4 * count:5 * count]
        return carry

    lax.fori_loop(0, N_TM, one, 0)


def lanes_of(tile):
    return slice(tile * 128, tile * 128 + 128)


def model_step(src, load, store, cf_sc, which):
    tiles = LON // 128
    lane = iota((32, 128), 1)
    at_first, at_last = lane == 0, lane == 127

    def ready(j):
        u = load(j)
        return u, pltpu.roll(u, 1, 1), pltpu.roll(u, 127, 1)

    before = ready(tiles - 1)
    first = now = ready(0)
    for j in range(tiles):
        after = first if j == tiles - 1 else ready(j + 1)
        lower = jnp.where(at_first, before[1], now[1])
        higher = jnp.where(at_last, after[2], now[2])
        cf = cf_sc.at[which]
        new = (cf[0, j] * now[0] + cf[1, j] * higher + cf[2, j] * lower
               + cf[3, j] * src[j, PAD + 1:PAD + 33, :] + cf[4, j] * src[j, PAD - 1:PAD + 31, :])
        store(j, new)
        before, now = now, after


def likelihood(f, lat, n_lat, xg_sc, halo_sc, cf_sc, cnt_sc, os_sc, fields, adj_sc):
    south = jnp.where(lat > 0, 1.0, 0.0).astype(F32)
    north = jnp.where(lat < n_lat - 1, 1.0, 0.0).astype(F32)
    for c in range(2):
        for j in range(LON // 128):
            here = lanes_of(j)
            ref = fields[c][1]
            ref[j, PAD:PAD + 8, :] = halo_sc[0, f, c, :, here].astype(F32) * south
            ref[j, PAD + 8:PAD + 24, :] = xg_sc[1, f, c, :, here].astype(F32)
            ref[j, PAD + 24:PAD + 32, :] = halo_sc[1, f, c, :, here].astype(F32) * north

    def store_to(ref, c, step):
        def store(j, new):
            if step == SUB - 1:
                ref[j, PAD:PAD + 32, :] = cnt_sc[f, j] * new - os_sc[f, c, j]
            elif step == 2 * SUB - 1:
                adj_sc[f, c, :, lanes_of(j)] = new[8:24]
            else:
                ref[j, PAD:PAD + 32, :] = new
        return store

    for step in range(2 * SUB):
        for c in range(2):
            src, dst = fields[c][1 - step % 2], fields[c][step % 2]
            model_step(src, lambda j: src[j, PAD:PAD + 32, :], store_to(dst, c, step), cf_sc, step // SUB)


def first_sums(n, xg_sc, hx_sc, rh_sc, w_sc, y_sc):
    base = pl.multiple_of(n * WIDTH, WIDTH)
    before = pl.multiple_of(lax.rem(n * WIDTH + LON - 128, LON), 128)
    after = pl.multiple_of(lax.rem(n * WIDTH + WIDTH, LON), 128)
    here = pl.ds(base, WIDTH)
    for piece in range(14):
        if piece < 12:
            g, f, c = piece // 4, (piece // 2) % 2, piece % 2
            load = lambda lanes: xg_sc[g, f, c, :, lanes]
        else:
            load = lambda lanes: hx_sc[(piece - 12) * 16:(piece - 11) * 16, lanes]
        rows = slice(piece * 16, piece * 16 + 16)
        mid = load(here)
        prev, nxt = load(pl.ds(before, 128)), load(pl.ds(after, 128))
        rh_sc[0, rows, :] = shift_lanes(jnp.concatenate([prev, mid], axis=1), 1)[:, 128:]
        rh_sc[1, rows, :] = mid
        rh_sc[2, rows, :] = shift_lanes(jnp.concatenate([mid, nxt], axis=1), WIDTH + 127)[:, :WIDTH]


def first_part(t, rh_sc, w_sc, y_sc):
    y = None
    for j in range(3):
        rhs = jnp.concatenate([rh_sc[j, t * 32:t * 32 + MAIN, :], rh_sc[j, 192:224, :]], axis=0)
        part = jnp.dot(w_sc[t, j], rhs, preferred_element_type=F32)
        y = part if y is None else y + part
    y_sc[t] = y


def finish_part(t, rb, n, y_sc, mix_sc, mixb_sc, out_sc, ob, adj_sc, out):
    here = pl.ds(pl.multiple_of(n * WIDTH, WIDTH), WIDTH)
    first = gelu_of_twice(y_sc[t, rb * 256:(rb + 1) * 256, :])
    z = jnp.dot(mix_sc[...], first, preferred_element_type=F32)
    z = (z.reshape(8, HID, WIDTH) + mixb_sc[...][None]).reshape(256, WIDTH)
    second = gelu_of_twice(z)
    o = jnp.dot(out_sc[...], second, preferred_element_type=F32)
    rows = slice(rb * 8, rb * 8 + 8)
    for c in range(2):
        out[t, c, rows, here] = o[c * 8:c * 8 + 8] + ob[0, c] - adj_sc[t, c, rows, here]


def shift_lanes(x, amount):
    return pltpu.roll(x, amount, 1)


def kernel(n_lat, bg, sens, obs, de, dn, dk, cw, cb, mw, mb, ow, ob, out,
           xg_sc, e_sc, h_sc, halo_sc, call_sc, sens_sc, obs_sc,
           hx_sc, cf_sc, cnt_sc, os_sc, adj_sc, ua_sc, ub_sc, uc_sc, ud_sc, rh_sc, y_sc, y2_sc, w_sc, mix_sc, mixb_sc, out_sc,
           loc, s_lat, r_lat, s_e, r_e, s_h, r_h, s_tm, r_tm, s_sl, r_sl, s_z, r_z, s_y, r_y, s_c, r_c):
    tm, lat = lax.axis_index("tm"), lax.axis_index("lat")
    z_hi = lax.rem(tm, 2)
    partner = tm + 1 - 2 * z_hi
    step_y = 2 - 4 * z_hi
    onward = lax.rem(tm + step_y + N_TM, N_TM)
    up, down = lax.rem(lat + 1, n_lat), lax.rem(lat + n_lat - 1, n_lat)
    from_partner = 2 - 2 * z_hi
    to_partner = 2 * z_hi

    def remote(src, dst, ss, rs, dev):
        return pltpu.make_async_remote_copy(src_ref=src, dst_ref=dst, send_sem=ss, recv_sem=rs, device_id=dev, device_id_type=MESH)

    own = pltpu.make_async_copy(bg, xg_sc.at[1], loc.at[0])
    own.start()
    own_sens = pltpu.make_async_copy(sens.at[pl.ds(2 * tm, 2)], sens_sc.at[1, tm], loc.at[1])
    own_sens.start()
    own_obs = pltpu.make_async_copy(obs.at[pl.ds(2 * tm, 2)], obs_sc.at[1, tm], loc.at[2])
    own_obs.start()
    for n, ref in enumerate((de, dn, dk)):
        val = ref[...] - (MID_K if n == 2 else 0.0)
        call_sc[tm, 1, n] = val[0:8].astype(BF16)
        call_sc[tm, 2, n] = val[8:16].astype(BF16)
    own.wait()
    half = LON // 2
    for e, row in ((0, 15), (1, 0)):
        rows = [xg_sc[1, f, c].astype(F32)[row:row + 1, :] for f in range(2) for c in range(2)]
        rows = [r[:, :half] for r in rows] + [r[:, half:] for r in rows]
        e_sc[e] = jnp.concatenate(rows, axis=0).astype(BF16)

    barrier = pltpu.get_barrier_semaphore()
    for d in range(1, N_TM):
        pl.semaphore_signal(barrier, inc=1, device_id=(lax.rem(tm + d, N_TM), lat), device_id_type=MESH)
    for other in (up, down):
        for who in (tm, partner):
            pl.semaphore_signal(barrier, inc=1, device_id=(who, other), device_id_type=MESH)
    build_weights(tm, lat, n_lat, cw, cb, mw, mb, ow, w_sc, mix_sc, mixb_sc, out_sc)
    pl.semaphore_wait(barrier, N_TM + 3)

    near = []
    for n, (dev, q_src, q_dst, e) in enumerate(((up, 2, 0, 0), (down, 1, 3, 1))):
        for w, (who, slot) in enumerate(((tm, 1), (partner, to_partner))):
            near.append(remote(call_sc.at[tm, q_src], call_sc.at[tm, q_dst], s_lat.at[n, w], r_lat.at[n, w], (who, dev)))
            near.append(remote(e_sc.at[e], h_sc.at[slot, e], s_e.at[n, w], r_e.at[n, w], (who, dev)))
    coef_z = remote(call_sc.at[tm, pl.ds(1, 2)], call_sc.at[tm, pl.ds(1, 2)], s_c.at[0], r_c.at[0], (partner, lat))
    coef_z.start()
    for cp in near:
        cp.start()
    tm_copies = []
    for d in range(1, N_TM):
        to = lax.rem(tm + d, N_TM)
        for m, (src, dst) in enumerate(((sens, sens_sc), (obs, obs_sc))):
            cp = remote(src.at[pl.ds(2 * to, 2)], dst.at[1, tm], s_tm.at[m, d - 1], r_tm.at[m, d - 1], (to, lat))
            cp.start()
            tm_copies.append(cp)
    halos = []
    for n, (dev, rows) in enumerate(((up, 8), (down, 0))):
        halos.append(remote(bg.at[:, :, pl.ds(rows, 8), :], halo_sc.at[n], s_h.at[n], r_h.at[n], (tm, dev)))
    frames = []
    for n in range(CHUNKS):
        lanes = pl.ds(n * WIDTH, WIDTH)
        frames.append(remote(bg.at[:, :, :, lanes], xg_sc.at[to_partner, :, :, :, lanes], s_z.at[n], r_z.at[n], (partner, lat)))
    order = [CHUNKS - 1] + list(range(CHUNKS - 1))
    for cp in halos + [frames[n] for n in order[:WINDOW]]:
        cp.start()

    def arrive(n):
        return remote(bg.at[:, :, :, pl.ds(0, WIDTH)], xg_sc.at[from_partner, :, :, :, lanes_at(n)], s_z.at[n], r_z.at[n], (partner, lat))

    def onto(n):
        return remote(xg_sc.at[from_partner, :, :, :, lanes_at(n)], xg_sc.at[to_partner, :, :, :, lanes_at(n)], s_y.at[n], r_y.at[n], (onward, lat))

    def relay(k):
        arrive(order[k]).wait_recv()
        onto(order[k]).start()
        if k + WINDOW < CHUNKS:
            frames[order[k + WINDOW]].start()

    for n, q_dst in enumerate((0, 3)):
        for w, who in enumerate((tm, partner)):
            there = call_sc.at[who, q_dst]
            remote(there, there, s_lat.at[n, w], r_lat.at[n, w], (partner, lat)).wait_recv()
    there = call_sc.at[partner, pl.ds(1, 2)]
    remote(there, there, s_c.at[0], r_c.at[0], (partner, lat)).wait_recv()
    coef_y = []
    pair = pl.ds(tm - z_hi, 2)
    for d in range(1, 4):
        cp = remote(call_sc.at[pair], call_sc.at[pair], s_c.at[d], r_c.at[d], (lax.rem(tm + 2 * d, N_TM), lat))
        cp.start()
        coef_y.append(cp)
    for n in range(2):
        for w, slot in enumerate((1, from_partner)):
            there = h_sc.at[slot, n]
            remote(there, there, s_e.at[n, w], r_e.at[n, w], (partner, lat)).wait_recv()
    edge_y = remote(h_sc.at[from_partner], h_sc.at[to_partner], s_y.at[CHUNKS], r_y.at[CHUNKS], (onward, lat))
    edge_y.start()
    relay(0)
    own_sens.wait()
    own_obs.wait()
    for d in range(1, N_TM):
        frm = lax.rem(tm - d + N_TM, N_TM)
        for m, (src, dst) in enumerate(((sens, sens_sc), (obs, obs_sc))):
            remote(src.at[pl.ds(0, 2)], dst.at[1, frm], s_tm.at[m, d - 1], r_tm.at[m, d - 1], (frm, lat)).wait_recv()
    sensor_copies = []
    for n, (dev, side) in enumerate(((up, 0), (down, 2))):
        for m, ref in enumerate((sens_sc, obs_sc)):
            cp = remote(ref.at[1], ref.at[side], s_sl.at[n, m], r_sl.at[n, m], (tm, dev))
            cp.start()
            sensor_copies.append(cp)
    relay(1)
    for cp in sensor_copies:
        cp.wait_recv()
    build_spread(sens_sc, obs_sc, cnt_sc, os_sc)
    relay(2)
    edge_y.wait_recv()
    build_edges(h_sc, hx_sc)
    relay(3)

    def conv_pairs(low, high):
        def two_chunks(m, carry):
            @pl.when(m == 1)
            def _():
                relay(7)
                onto(4).wait_recv()
                onto(5).wait_recv()

            @pl.when(m == 2)
            def _():
                onto(6).wait_recv()

            for odd in range(2):
                n = 2 * m + odd
                now, later = (y_sc, y2_sc) if odd == 0 else (y2_sc, y_sc)
                first_sums(jnp.minimum(n + 1, CHUNKS - 1), xg_sc, hx_sc, rh_sc, w_sc, later)
                for t in range(2):
                    first_part(t, rh_sc, w_sc, later)
                    for rb in range(2):
                        finish_part(t, rb, n, now, mix_sc, mixb_sc, out_sc, ob, adj_sc, out)
            return carry

        lax.fori_loop(low, high, two_chunks, 0)

    def conv_start():
        for n in order[:5]:
            onto(n).wait_recv()
        first_sums(0, xg_sc, hx_sc, rh_sc, w_sc, y_sc)
        for t in range(2):
            first_part(t, rh_sc, w_sc, y_sc)

    def finish_likelihood():
        for d in range(1, 4):
            there = pl.ds(lax.rem(tm - z_hi - 2 * d + N_TM, N_TM), 2)
            remote(call_sc.at[there], call_sc.at[there], s_c.at[d], r_c.at[d], (lax.rem(tm + 2 * d, N_TM), lat)).wait_recv()
        fields = ((ua_sc, ub_sc), (uc_sc, ud_sc))
        build_coefficients(lat, n_lat, call_sc, cf_sc, fields)
        for cp in halos:
            cp.wait_recv()

        def one_frame(f, carry):
            likelihood(f, lat, n_lat, xg_sc, halo_sc, cf_sc, cnt_sc, os_sc, fields, adj_sc)
            for n in range(2):
                @pl.when(f == n)
                def _():
                    relay(n + 4)
            return carry

        lax.fori_loop(0, 2, one_frame, 0)

    finish_likelihood()
    relay(6)
    conv_start()
    conv_pairs(0, CHUNKS // 2)

    for n in range(CHUNKS):
        onto(n).wait_send()
    for cp in near + halos + tm_copies + sensor_copies + frames + [coef_z, edge_y] + coef_y:
        cp.wait_send()


def lanes_at(n):
    return pl.ds(pl.multiple_of(n * WIDTH, WIDTH), WIDTH)


def solution(mesh):
    n_lat = mesh.shape["lat"]

    def shards(background, conv_weight, conv_bias, mix_weight, mix_bias, out_weight, out_bias,
               drift_east, drift_north, diffusivity, sensors, observations):
        vmem = pl.BlockSpec(memory_space=pltpu.VMEM)
        hbm = pl.BlockSpec(memory_space=pl.ANY)
        smem = pl.BlockSpec(memory_space=pltpu.SMEM)
        dma = pltpu.SemaphoreType.DMA
        scratch = [
            pltpu.VMEM((3, 2, 2, ROWS, LON), BF16),
            pltpu.VMEM((2, 8, LON // 2), BF16),
            pltpu.VMEM((3, 2, 8, LON // 2), BF16),
            pltpu.VMEM((2, 2, 2, 8, LON), BF16),
            pltpu.VMEM((N_TM, 4, 3, 8, TILE), BF16),
            pltpu.VMEM((3, N_TM, 2, 1, 1, 128), I32),
            pltpu.VMEM((3, N_TM, 2, 1, 1, 2, 128), F32),
            pltpu.VMEM((EXTRA, LON), BF16),
            pltpu.VMEM((2, 5, LON // 128, 32, 128), F32),
            pltpu.VMEM((2, LON // 128, 32, 128), F32),
            pltpu.VMEM((2, 2, LON // 128, 32, 128), F32),
            pltpu.VMEM((2, 2, ROWS, LON), F32),
            pltpu.VMEM((LON // 128, 32 + 2 * PAD, 128), F32),
            pltpu.VMEM((LON // 128, 32 + 2 * PAD, 128), F32),
            pltpu.VMEM((LON // 128, 32 + 2 * PAD, 128), F32),
            pltpu.VMEM((LON // 128, 32 + 2 * PAD, 128), F32),
            pltpu.VMEM((3, 224, WIDTH), BF16),
            pltpu.VMEM((2, ROWS * HID, WIDTH), F32),
            pltpu.VMEM((2, ROWS * HID, WIDTH), F32),
            pltpu.VMEM((2, 3, ROWS * HID, KDIM), BF16),
            pltpu.VMEM((256, 256), BF16),
            pltpu.VMEM((HID, WIDTH), F32),
            pltpu.VMEM((16, 256), BF16),
            dma((3,)), dma((2, 2)), dma((2, 2)), dma((2, 2)), dma((2, 2)), dma((2,)), dma((2,)), dma((2, 7)), dma((2, 7)), dma((2, 2)), dma((2, 2)),
            dma((CHUNKS + 1,)), dma((CHUNKS + 1,)), dma((CHUNKS + 1,)), dma((CHUNKS + 1,)), dma((4,)), dma((4,)),
        ]
        return pl.pallas_call(
            functools.partial(kernel, n_lat),
            out_shape=jax.ShapeDtypeStruct((2, 2, ROWS, LON), F32),
            in_specs=[hbm, hbm, hbm] + [vmem] * 8 + [smem],
            out_specs=vmem,
            scratch_shapes=scratch,
            compiler_params=pltpu.CompilerParams(collective_id=0, has_side_effects=True, vmem_limit_bytes=56 * 1024 * 1024),
        )(background, sensors, observations, drift_east, drift_north, diffusivity,
          conv_weight, conv_bias.reshape(1, HID), mix_weight, mix_bias.reshape(1, HID), out_weight, out_bias.reshape(1, 2))

    placed = (P("tm", None, "lat", None), P(), P(), P(), P(), P(), P(), P("lat", "tm"), P("lat", "tm"), P("lat", "tm"),
              P(None, "lat", "tm", None), P(None, "lat", "tm", None, None))
    return jax.shard_map(shards, mesh=mesh, in_specs=placed, out_specs=P("tm", None, "lat", None), check_vma=False)
```

```python
import functools

import jax
import jax.numpy as jnp
from jax import lax
from jax.experimental import pallas as pl
from jax.experimental.pallas import tpu as pltpu
from jax.sharding import PartitionSpec as P

MESH = pl.DeviceIdType.MESH
F32, BF16, I32 = jnp.float32, jnp.bfloat16, jnp.int32
N_TM = 8
ROWS, LON, TILE = 16, 2048, 256
HID, TAPS, KT, SUB = 32, 90, 5, 3
MID_K = 0.17
CHUNKS = 8
WIDTH = LON // CHUNKS
GELU_A = 1.5957691216057308
GELU_B = 0.2854192627
MAIN, EXTRA = 160, 32
KDIM = MAIN + EXTRA
PAD = 8
WINDOW = 4


def gelu_of_twice(y):
    t = jnp.tanh(y * (GELU_A + GELU_B * (y * y)))
    return (y + y * t).astype(BF16)


def iota(shape, dim):
    return lax.broadcasted_iota(I32, shape, dim)


def as_f32(mask):
    return jnp.where(mask, 1.0, 0.0).astype(F32)


def column(row):
    n = row.shape[1]
    eye = iota((n, n), 0) == iota((n, n), 1)
    return jnp.sum(jnp.where(eye, jnp.broadcast_to(row, (n, n)), 0.0), axis=1, keepdims=True)


def build_weights(tm, lat, n_lat, cw, cb, mw, mb, ow, w_sc, mix_sc, mixb_sc, out_sc):
    half_cw = (cw[...].astype(F32) * 0.5).astype(BF16)
    bias = column(cb[...] * 0.5)
    bias_hi = bias.astype(BF16).astype(F32)
    bias_lo = bias - bias_hi
    k = iota((1, KDIM), 1)
    main = k < MAIN
    kk = k - MAIN
    group_h, edge, f_h = kk // 8, (kk // 4) % 2, (kk // 2) % 2
    c = jnp.where(main, (k // 16) % 2, kk % 2)
    row_in = k % 16
    has_prev, has_next = tm > 0, tm < N_TM - 1
    has_south, has_north = lat > 0, lat < n_lat - 1
    bias_row = (as_f32(k == MAIN + 24) * bias_hi + as_f32(k == MAIN + 25) * bias_lo).astype(BF16)
    expanded = {}
    for t in range(2):
        lag = jnp.where(main, k // 32, 2 * group_h + f_h - t)
        group = (lag + t) // 2
        ok = (lag >= 0) & (lag < KT) & (main | (kk < 24))
        ok = ok & ((group > 0) | has_prev) & ((group < 2) | has_next)
        offset = iota((TAPS, KDIM), 0) - jnp.where(ok, (c * KT + lag) * 9, 1000)
        for j in range(3):
            for i in range(3):
                select = as_f32(offset == i * 3 + j).astype(BF16)
                expanded[t, j, i] = jnp.dot(half_cw, select, preferred_element_type=F32).astype(BF16)

    def one_row(r, carry):
        spot = [as_f32(main & (row_in == r + i - 1)) for i in range(3)]
        spot[0] = spot[0] + as_f32((~main) & (edge == 0) & (r == 0) & has_south)
        spot[2] = spot[2] + as_f32((~main) & (edge == 1) & (r == ROWS - 1) & has_north)
        spot = [jnp.broadcast_to(p, (HID, KDIM)).astype(BF16) for p in spot]
        for t in range(2):
            for j in range(3):
                val = expanded[t, j, 0] * spot[0] + expanded[t, j, 1] * spot[1] + expanded[t, j, 2] * spot[2]
                if j == 1:
                    val = val + bias_row
                w_sc[t, j, pl.ds(pl.multiple_of(r * HID, HID), HID), :] = val
        return carry

    lax.fori_loop(0, ROWS, one_row, 0)
    spread_lanes = as_f32(iota((HID, 8 * HID), 1) % HID == iota((HID, 8 * HID), 0)).astype(BF16)
    lane_row = iota((1, 8 * HID), 1) // HID
    mix_wide = jnp.dot((mw[...].astype(F32) * 0.5).astype(BF16), spread_lanes, preferred_element_type=F32)
    for r in range(8):
        mix_sc[r * HID:(r + 1) * HID, :] = (mix_wide * as_f32(lane_row == r)).astype(BF16)
    mixb_sc[...] = jnp.broadcast_to(column(mb[...] * 0.5), (HID, WIDTH))
    out_wide = jnp.dot(ow[...], spread_lanes, preferred_element_type=F32)
    own_row = iota((16, 8 * HID), 1) // HID == iota((16, 8 * HID), 0) % 8
    first_var = iota((16, 8 * HID), 0) < 8
    both = jnp.where(first_var, jnp.broadcast_to(out_wide[0:1], (16, 8 * HID)), jnp.broadcast_to(out_wide[1:2], (16, 8 * HID)))
    out_sc[...] = jnp.where(own_row, both, 0.0).astype(BF16)


def build_edges(h_sc, hx_sc):
    half = LON // 2
    for hf in range(2):
        parts = []
        for g in range(3):
            for e in range(2):
                parts.append(h_sc[g, e].astype(F32)[hf * 4:hf * 4 + 4, :])
        tail = as_f32(iota((8, half), 0) < 2)
        hx_sc[:, hf * half:(hf + 1) * half] = jnp.concatenate(parts + [tail], axis=0).astype(BF16)


def build_coefficients(lat, n_lat, call_sc, cf_sc, fields):
    for ref in fields[0] + fields[1]:
        for j in range(LON // 128):
            ref[j, 0:PAD, :] = jnp.zeros((PAD, 128), F32)
            ref[j, PAD + 32:, :] = jnp.zeros((PAD, 128), F32)
    lane = iota((32, 128), 1)
    live = jnp.where(lat > 0, 1.0, 0.0), jnp.where(lat < n_lat - 1, 1.0, 0.0)
    inside = jnp.concatenate([jnp.full((8, 128), live[0], F32), jnp.ones((16, 128), F32), jnp.full((8, 128), live[1], F32)], axis=0)

    def one_tile(j, carry):
        tile, lanes = j // 2, pl.ds(pl.multiple_of(lax.rem(j, 2) * 128, 128), 128)
        a, b, k = (jnp.concatenate([call_sc[tile, q, n, :, lanes].astype(F32) for q in range(4)], axis=0) for n in range(3))
        k = (k + MID_K) * inside
        a = a * (inside * 0.5)
        b = b * (inside * 0.5)
        center = inside - 4.0 * k
        cf_sc[0, 0, j] = center
        cf_sc[0, 1, j] = k - a
        cf_sc[0, 2, j] = k + a
        cf_sc[0, 3, j] = k - b
        cf_sc[0, 4, j] = k + b
        cf_sc[1, 0, j] = center
        cf_sc[1, 3, j] = pltpu.roll(k + b, 31, 0)
        cf_sc[1, 4, j] = pltpu.roll(k - b, 1, 0)
        return carry

    lax.fori_loop(0, LON // 128, one_tile, 0)

    def shifted(j, carry):
        tiles = LON // 128
        after, before = lax.rem(j + 1, tiles), lax.rem(j + tiles - 1, tiles)
        cf_sc[1, 1, j] = jnp.where(lane == 127, pltpu.roll(cf_sc[0, 2, after], 127, 1), pltpu.roll(cf_sc[0, 2, j], 127, 1))
        cf_sc[1, 2, j] = jnp.where(lane == 0, pltpu.roll(cf_sc[0, 1, before], 1, 1), pltpu.roll(cf_sc[0, 1, j], 1, 1))
        return carry

    lax.fori_loop(0, LON // 128, shifted, 0)


def build_spread(sens_sc, obs_sc, cnt_sc, os_sc):
    col = iota((TILE, 128), 0)
    sides = ((0, 8, 0, 8), (1, 16, 8, 0), (2, 8, 24, 0))

    def one(tile, carry):
        for f in range(2):
            for side, count, at, first_row in sides:
                cell = sens_sc[side, tile, f, 0]
                there = lax.shift_right_logical(cell, 8) - first_row
                pick = as_f32(jnp.broadcast_to(there, (count, 128)) == iota((count, 128), 0))
                value = obs_sc[side, tile, f, 0, 0]
                high = value.astype(BF16).astype(F32)
                low = value - high
                left = jnp.concatenate([pick, pick * high[0:1], pick * high[1:2], pick * low[0:1], pick * low[1:2]], axis=0).astype(BF16)
                right = as_f32(jnp.broadcast_to(cell & (TILE - 1), (TILE, 128)) == col).astype(BF16)
                total = lax.dot_general(left, right, (((1,), (1,)), ((), ())), preferred_element_type=F32)
                rows = slice(at, at + count)
                for h in range(2):
                    part = total[:, lanes_of(h)]
                    cnt_sc[f, 2 * tile + h, rows, :] = part[0:count]
                    os_sc[f, 0, 2 * tile + h, rows, :] = part[count:2 * count] + part[3 * count:4 * count]
                    os_sc[f, 1, 2 * tile + h, rows, :] = part[2 * count:3 * count] + part[4 * count:5 * count]
        return carry

    lax.fori_loop(0, N_TM, one, 0)


def lanes_of(tile):
    return slice(tile * 128, tile * 128 + 128)


def model_step(src, load, store, cf_sc, which):
    tiles = LON // 128
    lane = iota((32, 128), 1)
    at_first, at_last = lane == 0, lane == 127

    def ready(j):
        u = load(j)
        return u, pltpu.roll(u, 1, 1), pltpu.roll(u, 127, 1)

    before = ready(tiles - 1)
    first = now = ready(0)
    for j in range(tiles):
        after = first if j == tiles - 1 else ready(j + 1)
        lower = jnp.where(at_first, before[1], now[1])
        higher = jnp.where(at_last, after[2], now[2])
        cf = cf_sc.at[which]
        new = (cf[0, j] * now[0] + cf[1, j] * higher + cf[2, j] * lower
               + cf[3, j] * src[j, PAD + 1:PAD + 33, :] + cf[4, j] * src[j, PAD - 1:PAD + 31, :])
        store(j, new)
        before, now = now, after


def likelihood(f, lat, n_lat, xg_sc, halo_sc, cf_sc, cnt_sc, os_sc, fields, adj_sc):
    south = jnp.where(lat > 0, 1.0, 0.0).astype(F32)
    north = jnp.where(lat < n_lat - 1, 1.0, 0.0).astype(F32)
    for c in range(2):
        for j in range(LON // 128):
            here = lanes_of(j)
            ref = fields[c][1]
            ref[j, PAD:PAD + 8, :] = halo_sc[0, f, c, :, here].astype(F32) * south
            ref[j, PAD + 8:PAD + 24, :] = xg_sc[1, f, c, :, here].astype(F32)
            ref[j, PAD + 24:PAD + 32, :] = halo_sc[1, f, c, :, here].astype(F32) * north

    def store_to(ref, c, step):
        def store(j, new):
            if step == SUB - 1:
                ref[j, PAD:PAD + 32, :] = cnt_sc[f, j] * new - os_sc[f, c, j]
            elif step == 2 * SUB - 1:
                adj_sc[f, c, :, lanes_of(j)] = new[8:24]
            else:
                ref[j, PAD:PAD + 32, :] = new
        return store

    for step in range(2 * SUB):
        for c in range(2):
            src, dst = fields[c][1 - step % 2], fields[c][step % 2]
            model_step(src, lambda j: src[j, PAD:PAD + 32, :], store_to(dst, c, step), cf_sc, step // SUB)


def first_sums(n, xg_sc, hx_sc, rh_sc, w_sc, y_sc):
    base = pl.multiple_of(n * WIDTH, WIDTH)
    before = pl.multiple_of(lax.rem(n * WIDTH + LON - 128, LON), 128)
    after = pl.multiple_of(lax.rem(n * WIDTH + WIDTH, LON), 128)
    here = pl.ds(base, WIDTH)
    for piece in range(14):
        if piece < 12:
            g, f, c = piece // 4, (piece // 2) % 2, piece % 2
            load = lambda lanes: xg_sc[g, f, c, :, lanes]
        else:
            load = lambda lanes: hx_sc[(piece - 12) * 16:(piece - 11) * 16, lanes]
        rows = slice(piece * 16, piece * 16 + 16)
        mid = load(here)
        prev, nxt = load(pl.ds(before, 128)), load(pl.ds(after, 128))
        rh_sc[0, rows, :] = shift_lanes(jnp.concatenate([prev, mid], axis=1), 1)[:, 128:]
        rh_sc[1, rows, :] = mid
        rh_sc[2, rows, :] = shift_lanes(jnp.concatenate([mid, nxt], axis=1), WIDTH + 127)[:, :WIDTH]


def first_part(t, rh_sc, w_sc, y_sc):
    y = None
    for j in range(3):
        rhs = jnp.concatenate([rh_sc[j, t * 32:t * 32 + MAIN, :], rh_sc[j, 192:224, :]], axis=0)
        part = jnp.dot(w_sc[t, j], rhs, preferred_element_type=F32)
        y = part if y is None else y + part
    y_sc[t] = y


def finish_part(t, rb, n, y_sc, mix_sc, mixb_sc, out_sc, ob, adj_sc, out):
    here = pl.ds(pl.multiple_of(n * WIDTH, WIDTH), WIDTH)
    first = gelu_of_twice(y_sc[t, rb * 256:(rb + 1) * 256, :])
    z = jnp.dot(mix_sc[...], first, preferred_element_type=F32)
    z = (z.reshape(8, HID, WIDTH) + mixb_sc[...][None]).reshape(256, WIDTH)
    second = gelu_of_twice(z)
    o = jnp.dot(out_sc[...], second, preferred_element_type=F32)
    rows = slice(rb * 8, rb * 8 + 8)
    for c in range(2):
        out[t, c, rows, here] = o[c * 8:c * 8 + 8] + ob[0, c] - adj_sc[t, c, rows, here]


def shift_lanes(x, amount):
    return pltpu.roll(x, amount, 1)


def kernel(n_lat, bg, sens, obs, de, dn, dk, cw, cb, mw, mb, ow, ob, out,
           xg_sc, e_sc, h_sc, halo_sc, call_sc, sens_sc, obs_sc,
           hx_sc, cf_sc, cnt_sc, os_sc, adj_sc, ua_sc, ub_sc, uc_sc, ud_sc, rh_sc, y_sc, y2_sc, w_sc, mix_sc, mixb_sc, out_sc,
           loc, s_lat, r_lat, s_e, r_e, s_h, r_h, s_tm, r_tm, s_sl, r_sl, s_z, r_z, s_y, r_y, s_c, r_c):
    tm, lat = lax.axis_index("tm"), lax.axis_index("lat")
    z_hi = lax.rem(tm, 2)
    partner = tm + 1 - 2 * z_hi
    step_y = 2 - 4 * z_hi
    onward = lax.rem(tm + step_y + N_TM, N_TM)
    up, down = lax.rem(lat + 1, n_lat), lax.rem(lat + n_lat - 1, n_lat)
    from_partner = 2 - 2 * z_hi
    to_partner = 2 * z_hi

    def remote(src, dst, ss, rs, dev):
        return pltpu.make_async_remote_copy(src_ref=src, dst_ref=dst, send_sem=ss, recv_sem=rs, device_id=dev, device_id_type=MESH)

    own = pltpu.make_async_copy(bg, xg_sc.at[1], loc.at[0])
    own.start()
    own_sens = pltpu.make_async_copy(sens.at[pl.ds(2 * tm, 2)], sens_sc.at[1, tm], loc.at[1])
    own_sens.start()
    own_obs = pltpu.make_async_copy(obs.at[pl.ds(2 * tm, 2)], obs_sc.at[1, tm], loc.at[2])
    own_obs.start()
    for n, ref in enumerate((de, dn, dk)):
        val = ref[...] - (MID_K if n == 2 else 0.0)
        call_sc[tm, 1, n] = val[0:8].astype(BF16)
        call_sc[tm, 2, n] = val[8:16].astype(BF16)
    own.wait()
    half = LON // 2
    for e, row in ((0, 15), (1, 0)):
        rows = [xg_sc[1, f, c].astype(F32)[row:row + 1, :] for f in range(2) for c in range(2)]
        rows = [r[:, :half] for r in rows] + [r[:, half:] for r in rows]
        e_sc[e] = jnp.concatenate(rows, axis=0).astype(BF16)

    barrier = pltpu.get_barrier_semaphore()
    for d in range(1, N_TM):
        pl.semaphore_signal(barrier, inc=1, device_id=(lax.rem(tm + d, N_TM), lat), device_id_type=MESH)
    for other in (up, down):
        for who in (tm, partner):
            pl.semaphore_signal(barrier, inc=1, device_id=(who, other), device_id_type=MESH)
    build_weights(tm, lat, n_lat, cw, cb, mw, mb, ow, w_sc, mix_sc, mixb_sc, out_sc)
    pl.semaphore_wait(barrier, N_TM + 3)

    near = []
    for n, (dev, q_src, q_dst, e) in enumerate(((up, 2, 0, 0), (down, 1, 3, 1))):
        for w, (who, slot) in enumerate(((tm, 1), (partner, to_partner))):
            near.append(remote(call_sc.at[tm, q_src], call_sc.at[tm, q_dst], s_lat.at[n, w], r_lat.at[n, w], (who, dev)))
            near.append(remote(e_sc.at[e], h_sc.at[slot, e], s_e.at[n, w], r_e.at[n, w], (who, dev)))
    coef_z = remote(call_sc.at[tm, pl.ds(1, 2)], call_sc.at[tm, pl.ds(1, 2)], s_c.at[0], r_c.at[0], (partner, lat))
    coef_z.start()
    for cp in near:
        cp.start()
    tm_copies = []
    for d in range(1, N_TM):
        to = lax.rem(tm + d, N_TM)
        for m, (src, dst) in enumerate(((sens, sens_sc), (obs, obs_sc))):
            cp = remote(src.at[pl.ds(2 * to, 2)], dst.at[1, tm], s_tm.at[m, d - 1], r_tm.at[m, d - 1], (to, lat))
            cp.start()
            tm_copies.append(cp)
    halos = []
    for n, (dev, rows) in enumerate(((up, 8), (down, 0))):
        halos.append(remote(bg.at[:, :, pl.ds(rows, 8), :], halo_sc.at[n], s_h.at[n], r_h.at[n], (tm, dev)))
    frames = []
    for n in range(CHUNKS):
        lanes = pl.ds(n * WIDTH, WIDTH)
        frames.append(remote(bg.at[:, :, :, lanes], xg_sc.at[to_partner, :, :, :, lanes], s_z.at[n], r_z.at[n], (partner, lat)))
    order = [CHUNKS - 1] + list(range(CHUNKS - 1))
    for n in order[:WINDOW]:
        frames[n].start()

    def arrive(n):
        return remote(bg.at[:, :, :, pl.ds(0, WIDTH)], xg_sc.at[from_partner, :, :, :, lanes_at(n)], s_z.at[n], r_z.at[n], (partner, lat))

    def onto(n):
        return remote(xg_sc.at[from_partner, :, :, :, lanes_at(n)], xg_sc.at[to_partner, :, :, :, lanes_at(n)], s_y.at[n], r_y.at[n], (onward, lat))

    def relay(k):
        arrive(order[k]).wait_recv()
        onto(order[k]).start()

    for n, q_dst in enumerate((0, 3)):
        for w, who in enumerate((tm, partner)):
            there = call_sc.at[who, q_dst]
            remote(there, there, s_lat.at[n, w], r_lat.at[n, w], (partner, lat)).wait_recv()
    there = call_sc.at[partner, pl.ds(1, 2)]
    remote(there, there, s_c.at[0], r_c.at[0], (partner, lat)).wait_recv()
    coef_y = []
    pair = pl.ds(tm - z_hi, 2)
    for d in range(1, 4):
        cp = remote(call_sc.at[pair], call_sc.at[pair], s_c.at[d], r_c.at[d], (lax.rem(tm + 2 * d, N_TM), lat))
        cp.start()
        coef_y.append(cp)
    for n in range(2):
        for w, slot in enumerate((1, from_partner)):
            there = h_sc.at[slot, n]
            remote(there, there, s_e.at[n, w], r_e.at[n, w], (partner, lat)).wait_recv()
    edge_y = remote(h_sc.at[from_partner], h_sc.at[to_partner], s_y.at[CHUNKS], r_y.at[CHUNKS], (onward, lat))
    edge_y.start()
    relay(0)
    own_sens.wait()
    own_obs.wait()
    for d in range(1, N_TM):
        frm = lax.rem(tm - d + N_TM, N_TM)
        for m, (src, dst) in enumerate(((sens, sens_sc), (obs, obs_sc))):
            remote(src.at[pl.ds(0, 2)], dst.at[1, frm], s_tm.at[m, d - 1], r_tm.at[m, d - 1], (frm, lat)).wait_recv()
    sensor_copies = []
    for n, (dev, side) in enumerate(((up, 0), (down, 2))):
        for m, ref in enumerate((sens_sc, obs_sc)):
            cp = remote(ref.at[1], ref.at[side], s_sl.at[n, m], r_sl.at[n, m], (tm, dev))
            cp.start()
            sensor_copies.append(cp)
    for cp in halos + [frames[n] for n in order[WINDOW:]]:
        cp.start()
    relay(1)
    relay(2)
    for cp in sensor_copies:
        cp.wait_recv()
    build_spread(sens_sc, obs_sc, cnt_sc, os_sc)
    relay(3)
    edge_y.wait_recv()
    build_edges(h_sc, hx_sc)

    def conv_pairs(low, high):
        def two_chunks(m, carry):
            @pl.when(m == 1)
            def _():
                relay(7)
                onto(4).wait_recv()
                onto(5).wait_recv()

            @pl.when(m == 2)
            def _():
                onto(6).wait_recv()

            for odd in range(2):
                n = 2 * m + odd
                now, later = (y_sc, y2_sc) if odd == 0 else (y2_sc, y_sc)
                first_sums(jnp.minimum(n + 1, CHUNKS - 1), xg_sc, hx_sc, rh_sc, w_sc, later)
                for t in range(2):
                    first_part(t, rh_sc, w_sc, later)
                    for rb in range(2):
                        finish_part(t, rb, n, now, mix_sc, mixb_sc, out_sc, ob, adj_sc, out)
            return carry

        lax.fori_loop(low, high, two_chunks, 0)

    def conv_start():
        for n in order[:5]:
            onto(n).wait_recv()
        first_sums(0, xg_sc, hx_sc, rh_sc, w_sc, y_sc)
        for t in range(2):
            first_part(t, rh_sc, w_sc, y_sc)

    def finish_likelihood():
        for d in range(1, 4):
            there = pl.ds(lax.rem(tm - z_hi - 2 * d + N_TM, N_TM), 2)
            remote(call_sc.at[there], call_sc.at[there], s_c.at[d], r_c.at[d], (lax.rem(tm + 2 * d, N_TM), lat)).wait_recv()
        fields = ((ua_sc, ub_sc), (uc_sc, ud_sc))
        build_coefficients(lat, n_lat, call_sc, cf_sc, fields)
        for cp in halos:
            cp.wait_recv()

        def one_frame(f, carry):
            likelihood(f, lat, n_lat, xg_sc, halo_sc, cf_sc, cnt_sc, os_sc, fields, adj_sc)
            for n in range(2):
                @pl.when(f == n)
                def _():
                    relay(n + 4)
            return carry

        lax.fori_loop(0, 2, one_frame, 0)

    finish_likelihood()
    relay(6)
    conv_start()
    conv_pairs(0, CHUNKS // 2)

    for n in range(CHUNKS):
        onto(n).wait_send()
    for cp in near + halos + tm_copies + sensor_copies + frames + [coef_z, edge_y] + coef_y:
        cp.wait_send()


def lanes_at(n):
    return pl.ds(pl.multiple_of(n * WIDTH, WIDTH), WIDTH)


def solution(mesh):
    n_lat = mesh.shape["lat"]

    def shards(background, conv_weight, conv_bias, mix_weight, mix_bias, out_weight, out_bias,
               drift_east, drift_north, diffusivity, sensors, observations):
        vmem = pl.BlockSpec(memory_space=pltpu.VMEM)
        hbm = pl.BlockSpec(memory_space=pl.ANY)
        smem = pl.BlockSpec(memory_space=pltpu.SMEM)
        dma = pltpu.SemaphoreType.DMA
        scratch = [
            pltpu.VMEM((3, 2, 2, ROWS, LON), BF16),
            pltpu.VMEM((2, 8, LON // 2), BF16),
            pltpu.VMEM((3, 2, 8, LON // 2), BF16),
            pltpu.VMEM((2, 2, 2, 8, LON), BF16),
            pltpu.VMEM((N_TM, 4, 3, 8, TILE), BF16),
            pltpu.VMEM((3, N_TM, 2, 1, 1, 128), I32),
            pltpu.VMEM((3, N_TM, 2, 1, 1, 2, 128), F32),
            pltpu.VMEM((EXTRA, LON), BF16),
            pltpu.VMEM((2, 5, LON // 128, 32, 128), F32),
            pltpu.VMEM((2, LON // 128, 32, 128), F32),
            pltpu.VMEM((2, 2, LON // 128, 32, 128), F32),
            pltpu.VMEM((2, 2, ROWS, LON), F32),
            pltpu.VMEM((LON // 128, 32 + 2 * PAD, 128), F32),
            pltpu.VMEM((LON // 128, 32 + 2 * PAD, 128), F32),
            pltpu.VMEM((LON // 128, 32 + 2 * PAD, 128), F32),
            pltpu.VMEM((LON // 128, 32 + 2 * PAD, 128), F32),
            pltpu.VMEM((3, 224, WIDTH), BF16),
            pltpu.VMEM((2, ROWS * HID, WIDTH), F32),
            pltpu.VMEM((2, ROWS * HID, WIDTH), F32),
            pltpu.VMEM((2, 3, ROWS * HID, KDIM), BF16),
            pltpu.VMEM((256, 256), BF16),
            pltpu.VMEM((HID, WIDTH), F32),
            pltpu.VMEM((16, 256), BF16),
            dma((3,)), dma((2, 2)), dma((2, 2)), dma((2, 2)), dma((2, 2)), dma((2,)), dma((2,)), dma((2, 7)), dma((2, 7)), dma((2, 2)), dma((2, 2)),
            dma((CHUNKS + 1,)), dma((CHUNKS + 1,)), dma((CHUNKS + 1,)), dma((CHUNKS + 1,)), dma((4,)), dma((4,)),
        ]
        return pl.pallas_call(
            functools.partial(kernel, n_lat),
            out_shape=jax.ShapeDtypeStruct((2, 2, ROWS, LON), F32),
            in_specs=[hbm, hbm, hbm] + [vmem] * 8 + [smem],
            out_specs=vmem,
            scratch_shapes=scratch,
            compiler_params=pltpu.CompilerParams(collective_id=0, has_side_effects=True, vmem_limit_bytes=56 * 1024 * 1024),
        )(background, sensors, observations, drift_east, drift_north, diffusivity,
          conv_weight, conv_bias.reshape(1, HID), mix_weight, mix_bias.reshape(1, HID), out_weight, out_bias.reshape(1, 2))

    placed = (P("tm", None, "lat", None), P(), P(), P(), P(), P(), P(), P("lat", "tm"), P("lat", "tm"), P("lat", "tm"),
              P(None, "lat", "tm", None), P(None, "lat", "tm", None, None))
    return jax.shard_map(shards, mesh=mesh, in_specs=placed, out_specs=P("tm", None, "lat", None), check_vma=False)
```

```python
import functools

import jax
import jax.numpy as jnp
from jax import lax
from jax.experimental import pallas as pl
from jax.experimental.pallas import tpu as pltpu
from jax.sharding import PartitionSpec as P

MESH = pl.DeviceIdType.MESH
F32, BF16, I32 = jnp.float32, jnp.bfloat16, jnp.int32
N_TM = 8
ROWS, LON, TILE = 16, 2048, 256
HID, TAPS, KT, SUB = 32, 90, 5, 3
MID_K = 0.17
CHUNKS = 8
WIDTH = LON // CHUNKS
GELU_A = 1.5957691216057308
GELU_B = 0.2854192627
MAIN, EXTRA = 160, 32
KDIM = MAIN + EXTRA
PAD = 8
WINDOW = 4


def gelu_of_twice(y):
    t = jnp.tanh(y * (GELU_A + GELU_B * (y * y)))
    return (y + y * t).astype(BF16)


def iota(shape, dim):
    return lax.broadcasted_iota(I32, shape, dim)


def as_f32(mask):
    return jnp.where(mask, 1.0, 0.0).astype(F32)


def column(row):
    n = row.shape[1]
    eye = iota((n, n), 0) == iota((n, n), 1)
    return jnp.sum(jnp.where(eye, jnp.broadcast_to(row, (n, n)), 0.0), axis=1, keepdims=True)


def build_weights(tm, lat, n_lat, cw, cb, mw, mb, ow, w_sc, mix_sc, mixb_sc, out_sc):
    half_cw = (cw[...].astype(F32) * 0.5).astype(BF16)
    bias = column(cb[...] * 0.5)
    bias_hi = bias.astype(BF16).astype(F32)
    bias_lo = bias - bias_hi
    k = iota((1, KDIM), 1)
    main = k < MAIN
    kk = k - MAIN
    group_h, edge, f_h = kk // 8, (kk // 4) % 2, (kk // 2) % 2
    c = jnp.where(main, (k // 16) % 2, kk % 2)
    row_in = k % 16
    has_prev, has_next = tm > 0, tm < N_TM - 1
    has_south, has_north = lat > 0, lat < n_lat - 1
    bias_row = (as_f32(k == MAIN + 24) * bias_hi + as_f32(k == MAIN + 25) * bias_lo).astype(BF16)
    expanded = {}
    for t in range(2):
        lag = jnp.where(main, k // 32, 2 * group_h + f_h - t)
        group = (lag + t) // 2
        ok = (lag >= 0) & (lag < KT) & (main | (kk < 24))
        ok = ok & ((group > 0) | has_prev) & ((group < 2) | has_next)
        offset = iota((TAPS, KDIM), 0) - jnp.where(ok, (c * KT + lag) * 9, 1000)
        for j in range(3):
            for i in range(3):
                select = as_f32(offset == i * 3 + j).astype(BF16)
                expanded[t, j, i] = jnp.dot(half_cw, select, preferred_element_type=F32).astype(BF16)

    def one_row(r, carry):
        spot = [as_f32(main & (row_in == r + i - 1)) for i in range(3)]
        spot[0] = spot[0] + as_f32((~main) & (edge == 0) & (r == 0) & has_south)
        spot[2] = spot[2] + as_f32((~main) & (edge == 1) & (r == ROWS - 1) & has_north)
        spot = [jnp.broadcast_to(p, (HID, KDIM)).astype(BF16) for p in spot]
        for t in range(2):
            for j in range(3):
                val = expanded[t, j, 0] * spot[0] + expanded[t, j, 1] * spot[1] + expanded[t, j, 2] * spot[2]
                if j == 1:
                    val = val + bias_row
                w_sc[t, j, pl.ds(pl.multiple_of(r * HID, HID), HID), :] = val
        return carry

    lax.fori_loop(0, ROWS, one_row, 0)
    spread_lanes = as_f32(iota((HID, 8 * HID), 1) % HID == iota((HID, 8 * HID), 0)).astype(BF16)
    lane_row = iota((1, 8 * HID), 1) // HID
    mix_wide = jnp.dot((mw[...].astype(F32) * 0.5).astype(BF16), spread_lanes, preferred_element_type=F32)
    for r in range(8):
        mix_sc[r * HID:(r + 1) * HID, :] = (mix_wide * as_f32(lane_row == r)).astype(BF16)
    mixb_sc[...] = jnp.broadcast_to(column(mb[...] * 0.5), (HID, WIDTH))
    out_wide = jnp.dot(ow[...], spread_lanes, preferred_element_type=F32)
    own_row = iota((16, 8 * HID), 1) // HID == iota((16, 8 * HID), 0) % 8
    first_var = iota((16, 8 * HID), 0) < 8
    both = jnp.where(first_var, jnp.broadcast_to(out_wide[0:1], (16, 8 * HID)), jnp.broadcast_to(out_wide[1:2], (16, 8 * HID)))
    out_sc[...] = jnp.where(own_row, both, 0.0).astype(BF16)


def build_edges(h_sc, hx_sc):
    half = LON // 2
    for hf in range(2):
        parts = []
        for g in range(3):
            for e in range(2):
                parts.append(h_sc[g, e].astype(F32)[hf * 4:hf * 4 + 4, :])
        tail = as_f32(iota((8, half), 0) < 2)
        hx_sc[:, hf * half:(hf + 1) * half] = jnp.concatenate(parts + [tail], axis=0).astype(BF16)


def build_coefficients(lat, n_lat, call_sc, cf_sc, fields):
    for ref in fields[0] + fields[1]:
        for j in range(LON // 128):
            ref[j, 0:PAD, :] = jnp.zeros((PAD, 128), F32)
            ref[j, PAD + 32:, :] = jnp.zeros((PAD, 128), F32)
    lane = iota((32, 128), 1)
    live = jnp.where(lat > 0, 1.0, 0.0), jnp.where(lat < n_lat - 1, 1.0, 0.0)
    inside = jnp.concatenate([jnp.full((8, 128), live[0], F32), jnp.ones((16, 128), F32), jnp.full((8, 128), live[1], F32)], axis=0)

    def one_tile(j, carry):
        tile, lanes = j // 2, pl.ds(pl.multiple_of(lax.rem(j, 2) * 128, 128), 128)
        a, b, k = (jnp.concatenate([call_sc[tile, q, n, :, lanes].astype(F32) for q in range(4)], axis=0) for n in range(3))
        k = (k + MID_K) * inside
        a = a * (inside * 0.5)
        b = b * (inside * 0.5)
        center = inside - 4.0 * k
        cf_sc[0, 0, j] = center
        cf_sc[0, 1, j] = k - a
        cf_sc[0, 2, j] = k + a
        cf_sc[0, 3, j] = k - b
        cf_sc[0, 4, j] = k + b
        cf_sc[1, 0, j] = center
        cf_sc[1, 3, j] = pltpu.roll(k + b, 31, 0)
        cf_sc[1, 4, j] = pltpu.roll(k - b, 1, 0)
        return carry

    lax.fori_loop(0, LON // 128, one_tile, 0)

    def shifted(j, carry):
        tiles = LON // 128
        after, before = lax.rem(j + 1, tiles), lax.rem(j + tiles - 1, tiles)
        cf_sc[1, 1, j] = jnp.where(lane == 127, pltpu.roll(cf_sc[0, 2, after], 127, 1), pltpu.roll(cf_sc[0, 2, j], 127, 1))
        cf_sc[1, 2, j] = jnp.where(lane == 0, pltpu.roll(cf_sc[0, 1, before], 1, 1), pltpu.roll(cf_sc[0, 1, j], 1, 1))
        return carry

    lax.fori_loop(0, LON // 128, shifted, 0)


def build_spread(sens_sc, obs_sc, cnt_sc, os_sc):
    col = iota((TILE, 128), 0)
    sides = ((0, 8, 0, 8), (1, 16, 8, 0), (2, 8, 24, 0))

    def one(tile, carry):
        for f in range(2):
            for side, count, at, first_row in sides:
                cell = sens_sc[side, tile, f, 0]
                there = lax.shift_right_logical(cell, 8) - first_row
                pick = as_f32(jnp.broadcast_to(there, (count, 128)) == iota((count, 128), 0))
                value = obs_sc[side, tile, f, 0, 0]
                high = value.astype(BF16).astype(F32)
                low = value - high
                left = jnp.concatenate([pick, pick * high[0:1], pick * high[1:2], pick * low[0:1], pick * low[1:2]], axis=0).astype(BF16)
                right = as_f32(jnp.broadcast_to(cell & (TILE - 1), (TILE, 128)) == col).astype(BF16)
                total = lax.dot_general(left, right, (((1,), (1,)), ((), ())), preferred_element_type=F32)
                rows = slice(at, at + count)
                for h in range(2):
                    part = total[:, lanes_of(h)]
                    cnt_sc[f, 2 * tile + h, rows, :] = part[0:count]
                    os_sc[f, 0, 2 * tile + h, rows, :] = part[count:2 * count] + part[3 * count:4 * count]
                    os_sc[f, 1, 2 * tile + h, rows, :] = part[2 * count:3 * count] + part[4 * count:5 * count]
        return carry

    lax.fori_loop(0, N_TM, one, 0)


def lanes_of(tile):
    return slice(tile * 128, tile * 128 + 128)


def model_step(src, load, store, cf_sc, which):
    tiles = LON // 128
    lane = iota((32, 128), 1)
    at_first, at_last = lane == 0, lane == 127

    def ready(j):
        u = load(j)
        return u, pltpu.roll(u, 1, 1), pltpu.roll(u, 127, 1)

    before = ready(tiles - 1)
    first = now = ready(0)
    for j in range(tiles):
        after = first if j == tiles - 1 else ready(j + 1)
        lower = jnp.where(at_first, before[1], now[1])
        higher = jnp.where(at_last, after[2], now[2])
        cf = cf_sc.at[which]
        new = (cf[0, j] * now[0] + cf[1, j] * higher + cf[2, j] * lower
               + cf[3, j] * src[j, PAD + 1:PAD + 33, :] + cf[4, j] * src[j, PAD - 1:PAD + 31, :])
        store(j, new)
        before, now = now, after


def likelihood(f, lat, n_lat, xg_sc, halo_sc, cf_sc, cnt_sc, os_sc, fields, adj_sc):
    south = jnp.where(lat > 0, 1.0, 0.0).astype(F32)
    north = jnp.where(lat < n_lat - 1, 1.0, 0.0).astype(F32)
    for c in range(2):
        for j in range(LON // 128):
            here = lanes_of(j)
            ref = fields[c][1]
            ref[j, PAD:PAD + 8, :] = halo_sc[0, f, c, :, here].astype(F32) * south
            ref[j, PAD + 8:PAD + 24, :] = xg_sc[1, f, c, :, here].astype(F32)
            ref[j, PAD + 24:PAD + 32, :] = halo_sc[1, f, c, :, here].astype(F32) * north

    def store_to(ref, c, step):
        def store(j, new):
            if step == SUB - 1:
                ref[j, PAD:PAD + 32, :] = cnt_sc[f, j] * new - os_sc[f, c, j]
            elif step == 2 * SUB - 1:
                adj_sc[f, c, :, lanes_of(j)] = new[8:24]
            else:
                ref[j, PAD:PAD + 32, :] = new
        return store

    for step in range(2 * SUB):
        for c in range(2):
            src, dst = fields[c][1 - step % 2], fields[c][step % 2]
            model_step(src, lambda j: src[j, PAD:PAD + 32, :], store_to(dst, c, step), cf_sc, step // SUB)


def first_sums(n, xg_sc, hx_sc, rh_sc, w_sc, y_sc):
    base = pl.multiple_of(n * WIDTH, WIDTH)
    before = pl.multiple_of(lax.rem(n * WIDTH + LON - 128, LON), 128)
    after = pl.multiple_of(lax.rem(n * WIDTH + WIDTH, LON), 128)
    here = pl.ds(base, WIDTH)
    for piece in range(14):
        if piece < 12:
            g, f, c = piece // 4, (piece // 2) % 2, piece % 2
            load = lambda lanes: xg_sc[g, f, c, :, lanes]
        else:
            load = lambda lanes: hx_sc[(piece - 12) * 16:(piece - 11) * 16, lanes]
        rows = slice(piece * 16, piece * 16 + 16)
        mid = load(here)
        prev, nxt = load(pl.ds(before, 128)), load(pl.ds(after, 128))
        rh_sc[0, rows, :] = shift_lanes(jnp.concatenate([prev, mid], axis=1), 1)[:, 128:]
        rh_sc[1, rows, :] = mid
        rh_sc[2, rows, :] = shift_lanes(jnp.concatenate([mid, nxt], axis=1), WIDTH + 127)[:, :WIDTH]


def first_part(t, rh_sc, w_sc, y_sc):
    y = None
    for j in range(3):
        rhs = jnp.concatenate([rh_sc[j, t * 32:t * 32 + MAIN, :], rh_sc[j, 192:224, :]], axis=0)
        part = jnp.dot(w_sc[t, j], rhs, preferred_element_type=F32)
        y = part if y is None else y + part
    y_sc[t] = y


def finish_part(t, rb, n, y_sc, mix_sc, mixb_sc, out_sc, ob, adj_sc, out):
    here = pl.ds(pl.multiple_of(n * WIDTH, WIDTH), WIDTH)
    first = gelu_of_twice(y_sc[t, rb * 256:(rb + 1) * 256, :])
    z = jnp.dot(mix_sc[...], first, preferred_element_type=F32)
    z = (z.reshape(8, HID, WIDTH) + mixb_sc[...][None]).reshape(256, WIDTH)
    second = gelu_of_twice(z)
    o = jnp.dot(out_sc[...], second, preferred_element_type=F32)
    rows = slice(rb * 8, rb * 8 + 8)
    for c in range(2):
        out[t, c, rows, here] = o[c * 8:c * 8 + 8] + ob[0, c] - adj_sc[t, c, rows, here]


def shift_lanes(x, amount):
    return pltpu.roll(x, amount, 1)


def kernel(n_lat, bg, sens, obs, de, dn, dk, cw, cb, mw, mb, ow, ob, out,
           xg_sc, e_sc, h_sc, halo_sc, call_sc, sens_sc, obs_sc,
           hx_sc, cf_sc, cnt_sc, os_sc, adj_sc, ua_sc, ub_sc, uc_sc, ud_sc, rh_sc, y_sc, y2_sc, w_sc, mix_sc, mixb_sc, out_sc,
           loc, s_lat, r_lat, s_e, r_e, s_h, r_h, s_tm, r_tm, s_sl, r_sl, s_z, r_z, s_y, r_y, s_c, r_c):
    tm, lat = lax.axis_index("tm"), lax.axis_index("lat")
    z_hi = lax.rem(tm, 2)
    partner = tm + 1 - 2 * z_hi
    step_y = 2 - 4 * z_hi
    onward = lax.rem(tm + step_y + N_TM, N_TM)
    up, down = lax.rem(lat + 1, n_lat), lax.rem(lat + n_lat - 1, n_lat)
    from_partner = 2 - 2 * z_hi
    to_partner = 2 * z_hi

    def remote(src, dst, ss, rs, dev):
        return pltpu.make_async_remote_copy(src_ref=src, dst_ref=dst, send_sem=ss, recv_sem=rs, device_id=dev, device_id_type=MESH)

    own = pltpu.make_async_copy(bg, xg_sc.at[1], loc.at[0])
    own.start()
    own_sens = pltpu.make_async_copy(sens.at[pl.ds(2 * tm, 2)], sens_sc.at[1, tm], loc.at[1])
    own_sens.start()
    own_obs = pltpu.make_async_copy(obs.at[pl.ds(2 * tm, 2)], obs_sc.at[1, tm], loc.at[2])
    own_obs.start()
    for n, ref in enumerate((de, dn, dk)):
        val = ref[...] - (MID_K if n == 2 else 0.0)
        call_sc[tm, 1, n] = val[0:8].astype(BF16)
        call_sc[tm, 2, n] = val[8:16].astype(BF16)
    own.wait()
    half = LON // 2
    for e, row in ((0, 15), (1, 0)):
        rows = [xg_sc[1, f, c].astype(F32)[row:row + 1, :] for f in range(2) for c in range(2)]
        rows = [r[:, :half] for r in rows] + [r[:, half:] for r in rows]
        e_sc[e] = jnp.concatenate(rows, axis=0).astype(BF16)

    barrier = pltpu.get_barrier_semaphore()
    for d in range(1, N_TM):
        pl.semaphore_signal(barrier, inc=1, device_id=(lax.rem(tm + d, N_TM), lat), device_id_type=MESH)
    for other in (up, down):
        for who in (tm, partner):
            pl.semaphore_signal(barrier, inc=1, device_id=(who, other), device_id_type=MESH)
    build_weights(tm, lat, n_lat, cw, cb, mw, mb, ow, w_sc, mix_sc, mixb_sc, out_sc)
    pl.semaphore_wait(barrier, N_TM + 3)

    near = []
    for n, (dev, q_src, q_dst, e) in enumerate(((up, 2, 0, 0), (down, 1, 3, 1))):
        for w, (who, slot) in enumerate(((tm, 1), (partner, to_partner))):
            near.append(remote(call_sc.at[tm, q_src], call_sc.at[tm, q_dst], s_lat.at[n, w], r_lat.at[n, w], (who, dev)))
            near.append(remote(e_sc.at[e], h_sc.at[slot, e], s_e.at[n, w], r_e.at[n, w], (who, dev)))
    coef_z = remote(call_sc.at[tm, pl.ds(1, 2)], call_sc.at[tm, pl.ds(1, 2)], s_c.at[0], r_c.at[0], (partner, lat))
    coef_z.start()
    for cp in near:
        cp.start()
    tm_copies = []
    for d in range(1, N_TM):
        to = lax.rem(tm + d, N_TM)
        for m, (src, dst) in enumerate(((sens, sens_sc), (obs, obs_sc))):
            cp = remote(src.at[pl.ds(2 * to, 2)], dst.at[1, tm], s_tm.at[m, d - 1], r_tm.at[m, d - 1], (to, lat))
            cp.start()
            tm_copies.append(cp)
    halos = []
    for n, (dev, rows) in enumerate(((up, 8), (down, 0))):
        halos.append(remote(bg.at[:, :, pl.ds(rows, 8), :], halo_sc.at[n], s_h.at[n], r_h.at[n], (tm, dev)))
    frames = []
    for n in range(CHUNKS):
        lanes = pl.ds(n * WIDTH, WIDTH)
        frames.append(remote(xg_sc.at[1, :, :, :, lanes], xg_sc.at[to_partner, :, :, :, lanes], s_z.at[n], r_z.at[n], (partner, lat)))
    order = [CHUNKS - 1] + list(range(CHUNKS - 1))
    for n in order[:WINDOW]:
        frames[n].start()

    def arrive(n):
        return remote(bg.at[:, :, :, pl.ds(0, WIDTH)], xg_sc.at[from_partner, :, :, :, lanes_at(n)], s_z.at[n], r_z.at[n], (partner, lat))

    def onto(n):
        return remote(xg_sc.at[from_partner, :, :, :, lanes_at(n)], xg_sc.at[to_partner, :, :, :, lanes_at(n)], s_y.at[n], r_y.at[n], (onward, lat))

    def relay(k):
        arrive(order[k]).wait_recv()
        onto(order[k]).start()

    for n, q_dst in enumerate((0, 3)):
        for w, who in enumerate((tm, partner)):
            there = call_sc.at[who, q_dst]
            remote(there, there, s_lat.at[n, w], r_lat.at[n, w], (partner, lat)).wait_recv()
    there = call_sc.at[partner, pl.ds(1, 2)]
    remote(there, there, s_c.at[0], r_c.at[0], (partner, lat)).wait_recv()
    coef_y = []
    pair = pl.ds(tm - z_hi, 2)
    for d in range(1, 4):
        cp = remote(call_sc.at[pair], call_sc.at[pair], s_c.at[d], r_c.at[d], (lax.rem(tm + 2 * d, N_TM), lat))
        cp.start()
        coef_y.append(cp)
    for n in range(2):
        for w, slot in enumerate((1, from_partner)):
            there = h_sc.at[slot, n]
            remote(there, there, s_e.at[n, w], r_e.at[n, w], (partner, lat)).wait_recv()
    edge_y = remote(h_sc.at[from_partner], h_sc.at[to_partner], s_y.at[CHUNKS], r_y.at[CHUNKS], (onward, lat))
    edge_y.start()
    relay(0)
    own_sens.wait()
    own_obs.wait()
    for d in range(1, N_TM):
        frm = lax.rem(tm - d + N_TM, N_TM)
        for m, (src, dst) in enumerate(((sens, sens_sc), (obs, obs_sc))):
            remote(src.at[pl.ds(0, 2)], dst.at[1, frm], s_tm.at[m, d - 1], r_tm.at[m, d - 1], (frm, lat)).wait_recv()
    sensor_copies = []
    for n, (dev, side) in enumerate(((up, 0), (down, 2))):
        for m, ref in enumerate((sens_sc, obs_sc)):
            cp = remote(ref.at[1], ref.at[side], s_sl.at[n, m], r_sl.at[n, m], (tm, dev))
            cp.start()
            sensor_copies.append(cp)
    for cp in halos + [frames[n] for n in order[WINDOW:]]:
        cp.start()
    relay(1)
    relay(2)
    for cp in sensor_copies:
        cp.wait_recv()
    build_spread(sens_sc, obs_sc, cnt_sc, os_sc)
    relay(3)
    edge_y.wait_recv()
    build_edges(h_sc, hx_sc)

    def conv_pairs(low, high):
        def two_chunks(m, carry):
            @pl.when(m == 1)
            def _():
                relay(7)
                onto(4).wait_recv()
                onto(5).wait_recv()

            @pl.when(m == 2)
            def _():
                onto(6).wait_recv()

            for odd in range(2):
                n = 2 * m + odd
                now, later = (y_sc, y2_sc) if odd == 0 else (y2_sc, y_sc)
                first_sums(jnp.minimum(n + 1, CHUNKS - 1), xg_sc, hx_sc, rh_sc, w_sc, later)
                for t in range(2):
                    first_part(t, rh_sc, w_sc, later)
                    for rb in range(2):
                        finish_part(t, rb, n, now, mix_sc, mixb_sc, out_sc, ob, adj_sc, out)
            return carry

        lax.fori_loop(low, high, two_chunks, 0)

    def conv_start():
        for n in order[:5]:
            onto(n).wait_recv()
        first_sums(0, xg_sc, hx_sc, rh_sc, w_sc, y_sc)
        for t in range(2):
            first_part(t, rh_sc, w_sc, y_sc)

    def finish_likelihood():
        for d in range(1, 4):
            there = pl.ds(lax.rem(tm - z_hi - 2 * d + N_TM, N_TM), 2)
            remote(call_sc.at[there], call_sc.at[there], s_c.at[d], r_c.at[d], (lax.rem(tm + 2 * d, N_TM), lat)).wait_recv()
        fields = ((ua_sc, ub_sc), (uc_sc, ud_sc))
        build_coefficients(lat, n_lat, call_sc, cf_sc, fields)
        for cp in halos:
            cp.wait_recv()

        def one_frame(f, carry):
            likelihood(f, lat, n_lat, xg_sc, halo_sc, cf_sc, cnt_sc, os_sc, fields, adj_sc)
            for n in range(2):
                @pl.when(f == n)
                def _():
                    relay(n + 4)
            return carry

        lax.fori_loop(0, 2, one_frame, 0)

    finish_likelihood()
    relay(6)
    conv_start()
    conv_pairs(0, CHUNKS // 2)

    for n in range(CHUNKS):
        onto(n).wait_send()
    for cp in near + halos + tm_copies + sensor_copies + frames + [coef_z, edge_y] + coef_y:
        cp.wait_send()


def lanes_at(n):
    return pl.ds(pl.multiple_of(n * WIDTH, WIDTH), WIDTH)


def solution(mesh):
    n_lat = mesh.shape["lat"]

    def shards(background, conv_weight, conv_bias, mix_weight, mix_bias, out_weight, out_bias,
               drift_east, drift_north, diffusivity, sensors, observations):
        vmem = pl.BlockSpec(memory_space=pltpu.VMEM)
        hbm = pl.BlockSpec(memory_space=pl.ANY)
        smem = pl.BlockSpec(memory_space=pltpu.SMEM)
        dma = pltpu.SemaphoreType.DMA
        scratch = [
            pltpu.VMEM((3, 2, 2, ROWS, LON), BF16),
            pltpu.VMEM((2, 8, LON // 2), BF16),
            pltpu.VMEM((3, 2, 8, LON // 2), BF16),
            pltpu.VMEM((2, 2, 2, 8, LON), BF16),
            pltpu.VMEM((N_TM, 4, 3, 8, TILE), BF16),
            pltpu.VMEM((3, N_TM, 2, 1, 1, 128), I32),
            pltpu.VMEM((3, N_TM, 2, 1, 1, 2, 128), F32),
            pltpu.VMEM((EXTRA, LON), BF16),
            pltpu.VMEM((2, 5, LON // 128, 32, 128), F32),
            pltpu.VMEM((2, LON // 128, 32, 128), F32),
            pltpu.VMEM((2, 2, LON // 128, 32, 128), F32),
            pltpu.VMEM((2, 2, ROWS, LON), F32),
            pltpu.VMEM((LON // 128, 32 + 2 * PAD, 128), F32),
            pltpu.VMEM((LON // 128, 32 + 2 * PAD, 128), F32),
            pltpu.VMEM((LON // 128, 32 + 2 * PAD, 128), F32),
            pltpu.VMEM((LON // 128, 32 + 2 * PAD, 128), F32),
            pltpu.VMEM((3, 224, WIDTH), BF16),
            pltpu.VMEM((2, ROWS * HID, WIDTH), F32),
            pltpu.VMEM((2, ROWS * HID, WIDTH), F32),
            pltpu.VMEM((2, 3, ROWS * HID, KDIM), BF16),
            pltpu.VMEM((256, 256), BF16),
            pltpu.VMEM((HID, WIDTH), F32),
            pltpu.VMEM((16, 256), BF16),
            dma((3,)), dma((2, 2)), dma((2, 2)), dma((2, 2)), dma((2, 2)), dma((2,)), dma((2,)), dma((2, 7)), dma((2, 7)), dma((2, 2)), dma((2, 2)),
            dma((CHUNKS + 1,)), dma((CHUNKS + 1,)), dma((CHUNKS + 1,)), dma((CHUNKS + 1,)), dma((4,)), dma((4,)),
        ]
        return pl.pallas_call(
            functools.partial(kernel, n_lat),
            out_shape=jax.ShapeDtypeStruct((2, 2, ROWS, LON), F32),
            in_specs=[hbm, hbm, hbm] + [vmem] * 8 + [smem],
            out_specs=vmem,
            scratch_shapes=scratch,
            compiler_params=pltpu.CompilerParams(collective_id=0, has_side_effects=True, vmem_limit_bytes=56 * 1024 * 1024),
        )(background, sensors, observations, drift_east, drift_north, diffusivity,
          conv_weight, conv_bias.reshape(1, HID), mix_weight, mix_bias.reshape(1, HID), out_weight, out_bias.reshape(1, 2))

    placed = (P("tm", None, "lat", None), P(), P(), P(), P(), P(), P(), P("lat", "tm"), P("lat", "tm"), P("lat", "tm"),
              P(None, "lat", "tm", None), P(None, "lat", "tm", None, None))
    return jax.shard_map(shards, mesh=mesh, in_specs=placed, out_specs=P("tm", None, "lat", None), check_vma=False)
```
